512 devices in a mesh: seq: 128 (over x, z, y_hi), tp: 4 (over y_lo, core).
Axes of the slice: x: 4, y: 8 (y_hi: 4, y_lo: 2; y = y_hi * 2 + y_lo), z: 8, core: 2. Of those that a mesh axis runs over, the one named last changes fastest.
Arguments:
- residual_in: float32 [32768, 2048], P('seq', 'tp'), may hold values from -18 to 18
- query_rows: bfloat16 [32768, 2048], P('seq', 'tp'), may hold values from -6 to 6
- key_rows: bfloat16 [32768, 2048], P('seq', 'tp'), may hold values from -6 to 6
- value_rows: bfloat16 [32768, 2048], P('seq', 'tp'), may hold values from -6 to 6
- lengths: int32 [256], P('seq'), may hold values from 0 to 128, as said below
- norm_gain: float32 [2048], P('tp'), may hold values from 0.1 to 1.9
- gate_weight: bfloat16 [2048, 4096], P('seq', 'tp'), may hold values from -0.125 to 0.125
- up_weight: bfloat16 [2048, 4096], P('seq', 'tp'), may hold values from -0.125 to 0.125
- down_weight: bfloat16 [4096, 2048], P('tp', 'seq'), may hold values from -0.375 to 0.375
Outputs:
- attended: bfloat16 [32768, 2048], P('seq', 'tp')
- mixed: float32 [32768, 2048], P('seq', 'tp')
The draws below stay inside these ranges and needn't reach their ends.
Inputs may be any that keep to these rules, and one draw needn't show every extreme that they name: `lengths`: entry s counts the valid events at the start of segment s, the events s * 128 to s * 128 + 127; the rest of the segment is padding.
All inputs are finite; a program needn't handle non-finite values.
Results may differ from the reference program's by a relative error of at most 0.008.
Values may be sent and summed in bfloat16 or wider, within the bound.
No kernel may reach another device: no remote copies, remote signals or barrier semaphores. Data moves between devices by JAX's collectives and lax.ppermute only.
A program may use at most 64 MiB of HBM per device.

```python
import math
import jax
import jax.numpy as jnp
from jax import lax

D = 2048
HEADS = 16
HEAD_DIM = 128
FF = 4096
ROWS = 256
SEG = 128
WINDOW = 512
EVENTS = 32768
NSEG = 256
N_TP = 4


def draw_lengths(key, part):
    key_base, key_level, key_full, key_empty = jax.random.split(key, 4)
    per_device = ROWS // SEG
    base_counts = jax.random.randint(key_base, (NSEG,), 0, SEG + 1)
    levels = jax.random.randint(key_level, (NSEG // per_device,), 1, 5)
    spread = jnp.repeat(levels, per_device, total_repeat_length=NSEG)
    counts = base_counts * spread // 4
    full_index = jax.random.randint(key_full, (), 0, NSEG)
    empty_index = (full_index + 1 + jax.random.randint(key_empty, (), 0, NSEG - 1)) % NSEG
    counts = counts.at[full_index].set(SEG).at[empty_index].set(0)
    return counts.astype(jnp.int32)


def draw_query_rows(key, part):
    normal_part = jax.random.normal(jax.random.fold_in(key, 1), (EVENTS, D), jnp.float32)
    return jnp.clip(normal_part, -6.0, 6.0).astype(jnp.bfloat16)


def draw_key_rows(key, part):
    normal_part = jax.random.normal(jax.random.fold_in(key, 3), (EVENTS, D), jnp.float32)
    return jnp.clip(normal_part, -6.0, 6.0).astype(jnp.bfloat16)


def draw_residual_in(key, part):
    key_noise, key_column, key_row = jax.random.split(jax.random.fold_in(key, 11), 3)
    column = jnp.arange(D, dtype=jnp.float32) / D
    column_factor = jnp.exp(jax.random.uniform(key_column, (D,), jnp.float32, -0.35, 0.35))
    row_factor = jnp.exp(jax.random.uniform(key_row, (EVENTS, 1), jnp.float32, -0.5, 0.5))
    noise_part = jnp.clip(jax.random.normal(key_noise, (EVENTS, D), jnp.float32), -5.0, 5.0)
    rising = 0.3 * jnp.power(5.0, column)
    return noise_part * (rising * column_factor)[None, :] * row_factor


def spiked(array, own_key, source, target, parts, factor):
    owner, partner = [(jnp.arange(array.shape[axis_at]) // (array.shape[axis_at] // parts)).reshape([-1 if axis == axis_at else 1 for axis in range(array.ndim)]) for axis_at in (source, target)]
    chosen = jax.random.permutation(own_key, parts)[partner]
    strong = (owner == chosen) | (owner == (partner + parts // 2) % parts)
    return jnp.where(strong, factor * array, array)


def shard_levels(rng, extent, cuts, smallest, largest):
    def one(dim, blocks):
        heights = jax.random.uniform(jax.random.fold_in(jax.random.fold_in(rng, 6), dim), (blocks,), jnp.float32, smallest / len(cuts), largest / len(cuts))
        return jnp.repeat(jnp.exp(heights), extent[dim] // blocks).reshape((-1,) + (1,) * (len(extent) - dim - 1))

    loudness = one(*cuts[0])
    for cut in cuts[1:]:
        loudness = loudness * one(*cut)
    return loudness


def centred(rng, shape, scale, most, pieces=(), kind=jnp.bfloat16):
    values = scale * jax.random.normal(rng, shape, jnp.float32)
    if pieces:
        values = values * shard_levels(rng, shape, pieces, -0.22, 0.18)
    return jnp.clip(values, -most, most).astype(kind)


def gaussian_with(own_key, dims, deviation, reach, cuts, heavy, kind=jnp.bfloat16):
    result = deviation * jax.random.normal(own_key, dims, jnp.float32)
    if cuts:
        result = result * shard_levels(own_key, dims, cuts, -0.22, 0.18)
    return jnp.clip(spiked(result, jax.random.fold_in(own_key, 3), *heavy), -reach, reach).astype(kind)


def setup_inputs(seed: int = 0) -> dict:
    arg_keys = jax.random.split(jax.random.key(seed), 10)
    residual_in = draw_residual_in(jax.random.fold_in(arg_keys[9], 71), 0)
    query_rows = draw_query_rows(jax.random.fold_in(arg_keys[9], 71), 0)
    key_rows = draw_key_rows(jax.random.fold_in(arg_keys[9], 71), 0)
    value_rows = centred(arg_keys[3], (EVENTS, D), 1.0, 6.0, ((0, 128), (1, 4)))
    lengths = draw_lengths(jax.random.fold_in(arg_keys[9], 71), 0)
    norm_gain = jnp.clip(1.0 + 0.18 * jax.random.normal(arg_keys[5], (D,), jnp.float32), 0.1, 1.9)
    gate_weight = centred(arg_keys[6], (D, FF), D ** -0.5, 0.125, ((0, 128), (1, 4)))
    up_weight = centred(arg_keys[7], (D, FF), D ** -0.5, 0.125, ((0, 128), (1, 4)))
    down_weight = gaussian_with(arg_keys[8], (FF, D), FF ** -0.5, 0.375, ((0, 4), (1, 128)), (0, 1, 128, 5.5))
    return dict(residual_in=residual_in, query_rows=query_rows, key_rows=key_rows, value_rows=value_rows, lengths=lengths, norm_gain=norm_gain, gate_weight=gate_weight, up_weight=up_weight, down_weight=down_weight)


epsilon = 1e-06

def reference(residual_in, query_rows, key_rows, value_rows, lengths, norm_gain, gate_weight, up_weight, down_weight):
    total_rows = query_rows.shape[0]
    reach_blocks = (WINDOW + ROWS - 2) // ROWS
    key_span = (reach_blocks + 1) * ROWS
    front_pad = reach_blocks * ROWS
    offsets = jnp.arange(total_rows, dtype=jnp.int32) % SEG
    valid_mask = (offsets < jnp.repeat(lengths, SEG, total_repeat_length=total_rows)).astype(jnp.float32)
    key_pad = jnp.pad(key_rows, ((front_pad, 0), (0, 0)))
    value_pad = jnp.pad(value_rows, ((front_pad, 0), (0, 0)))
    valid_pad = jnp.pad(valid_mask, (front_pad, 0))
    block_count = total_rows // ROWS
    score_scale = 1.0 / math.sqrt(HEAD_DIM)
    group_size = FF // N_TP

    def one_block(block_index):
        block_start = (block_index * ROWS).astype(jnp.int32)
        query_block = lax.dynamic_slice_in_dim(query_rows, block_start, ROWS, 0).astype(jnp.float32).reshape(ROWS, HEADS, HEAD_DIM)
        key_block = lax.dynamic_slice_in_dim(key_pad, block_start, key_span, 0).astype(jnp.float32).reshape(key_span, HEADS, HEAD_DIM)
        value_block = lax.dynamic_slice_in_dim(value_pad, block_start, key_span, 0).astype(jnp.float32).reshape(key_span, HEADS, HEAD_DIM)
        key_valid = lax.dynamic_slice_in_dim(valid_pad, block_start, key_span, 0)
        query_valid = lax.dynamic_slice_in_dim(valid_mask, block_start, ROWS, 0)
        query_pos = block_start + jnp.arange(ROWS, dtype=jnp.int32)
        key_pos = block_start - front_pad + jnp.arange(key_span, dtype=jnp.int32)
        allowed = (key_pos[None, :] <= query_pos[:, None]) & (key_pos[None, :] > query_pos[:, None] - WINDOW)
        allowed = allowed & (key_pos[None, :] >= 0) & (key_valid[None, :] > 0)
        scores = jnp.einsum('qhd,khd->hqk', query_block, key_block) * score_scale
        masked = jnp.where(allowed[None], scores, -1e+30)
        row_max = lax.optimization_barrier(jnp.max(masked, axis=2, keepdims=True))
        weights = jnp.where(allowed[None], jnp.exp(masked - row_max), 0.0)
        denominator = lax.optimization_barrier(jnp.sum(weights, axis=2, keepdims=True))
        rounded = lax.optimization_barrier(weights.astype(jnp.bfloat16)).astype(jnp.float32)
        numerator = jnp.einsum('hqk,khd->hqd', rounded, value_block)
        keep_rows = query_valid[None, :, None] > 0
        head_out = jnp.where(keep_rows, numerator / jnp.where(keep_rows, denominator, 1.0), 0.0)
        attended = jnp.transpose(head_out, (1, 0, 2)).reshape(ROWS, HEADS * HEAD_DIM).astype(jnp.bfloat16)
        residual = lax.dynamic_slice_in_dim(residual_in, block_start, ROWS, 0) + attended.astype(jnp.float32)
        inverse = lax.rsqrt(lax.optimization_barrier(jnp.sum(residual * residual, axis=1, keepdims=True)) / D + epsilon)
        normed = (residual * inverse * norm_gain[None, :]).astype(jnp.bfloat16)
        gate_sum = jnp.dot(normed, gate_weight, preferred_element_type=jnp.float32)
        up_sum = jnp.dot(normed, up_weight, preferred_element_type=jnp.float32)
        hidden = (jax.nn.silu(gate_sum) * up_sum).astype(jnp.bfloat16)
        hidden_groups = hidden.astype(jnp.float32).reshape(ROWS, N_TP, group_size)
        down_groups = down_weight.astype(jnp.float32).reshape(N_TP, group_size, D)
        partials = jnp.einsum('rtg,tgd->trd', hidden_groups, down_groups)
        partials_rounded = lax.optimization_barrier(partials.astype(jnp.bfloat16)).astype(jnp.float32)
        mixed_block = residual + lax.optimization_barrier(jnp.sum(partials_rounded, axis=0))
        return (attended, mixed_block)
    attended_blocks, mixed_blocks = lax.map(one_block, jnp.arange(block_count, dtype=jnp.int32))
    return (attended_blocks.reshape(total_rows, D), mixed_blocks.reshape(total_rows, D))
```

```python
import math

import jax
import jax.numpy as jnp
from jax import lax
from jax.experimental import pallas as pl
from jax.experimental.pallas import tpu as pltpu
from jax.sharding import Mesh
from jax.sharding import PartitionSpec as P

D = 2048
HEAD_DIM = 128
SEG = 128
ROWS = 256
TP_WIDTH = 512
UNIT_BLOCK = 256
epsilon = 1e-06

SEQ = ("x", "z", "yh")
TP = ("yl", "c")
F32 = jnp.float32
BF16 = jnp.bfloat16


def from_behind(value, by):
    size = lax.axis_size(SEQ)
    return lax.ppermute(value, SEQ, [(i, i + by) for i in range(size - by)])


def swap(value, axis):
    return lax.ppermute(value, axis, [(0, 1), (1, 0)])


def attention_kernel(
    lengths_ref, q_ref, k0_ref, v0_ref, k1_ref, v1_ref, k2_ref, v2_ref, res_ref, att_ref, send_ref
):
    rows = lax.broadcasted_iota(jnp.int32, (ROWS, ROWS), 0)
    cols = lax.broadcasted_iota(jnp.int32, (ROWS, ROWS), 1)

    def valid(index, block):
        low = index < SEG
        bound = jnp.where(low, lengths_ref[2 * block], lengths_ref[2 * block + 1] + SEG)
        return index < bound

    allowed = (
        valid(cols, 0) & (cols <= rows),
        valid(cols, 1),
        valid(cols, 2) & (cols > rows),
    )
    keep = valid(lax.broadcasted_iota(jnp.int32, (ROWS, 1), 0), 0)
    scale = 1.0 / math.sqrt(HEAD_DIM)
    keys = (k0_ref, k1_ref, k2_ref)
    values = (v0_ref, v1_ref, v2_ref)
    for head in range(TP_WIDTH // HEAD_DIM):
        at = pl.ds(head * HEAD_DIM, HEAD_DIM)
        query = q_ref[:, at]
        masked = []
        for key_ref, allow in zip(keys, allowed):
            scores = lax.dot_general(
                query, key_ref[:, at], (((1,), (1,)), ((), ())), preferred_element_type=F32
            )
            masked.append(jnp.where(allow, scores * scale, -1e30))
        top = jnp.max(jnp.maximum(jnp.maximum(masked[0], masked[1]), masked[2]), axis=1, keepdims=True)
        weights = [jnp.where(a, jnp.exp(m - top), 0.0) for a, m in zip(allowed, masked)]
        denominator = jnp.sum(weights[0] + weights[1] + weights[2], axis=1, keepdims=True)
        numerator = jnp.zeros((ROWS, HEAD_DIM), F32)
        for weight, value_ref in zip(weights, values):
            numerator += jnp.dot(weight.astype(BF16), value_ref[:, at], preferred_element_type=F32)
        out = jnp.where(keep, numerator / jnp.where(keep, denominator, 1.0), 0.0).astype(BF16)
        att_ref[:, at] = out
        send_ref[:, at] = (res_ref[:, at] + out.astype(F32)).astype(BF16)


def attention(lengths, q, k0, v0, k1, v1, k2, v2, residual_in):
    vmem = pl.BlockSpec(memory_space=pltpu.VMEM)
    shape = jax.ShapeDtypeStruct(q.shape, BF16)
    return pl.pallas_call(
        attention_kernel,
        out_shape=(shape, shape),
        in_specs=[pl.BlockSpec(memory_space=pltpu.SMEM)] + [vmem] * 8,
        out_specs=(vmem, vmem),
        compiler_params=pltpu.CompilerParams(vmem_limit_bytes=32 << 20),
        cost_estimate=pl.CostEstimate(
            flops=4 * ROWS * 3 * ROWS * TP_WIDTH, bytes_accessed=3 << 20, transcendentals=3 << 18
        ),
        name="attention",
    )(lengths, q, k0, v0, k1, v1, k2, v2, residual_in)


def feed_forward_kernel(order_ref, r0, r1, r2, r3, gain_ref, w_ref, out_ref, x_ref, acc_ref):
    step = pl.program_id(0)
    parts = (r0, r1, r2, r3)

    @pl.when(step == 0)
    def _():
        square = jnp.zeros((ROWS, 1), F32)
        for ref in parts:
            value = ref[...].astype(F32)
            square += jnp.sum(value * value, axis=1, keepdims=True)
        inverse = lax.rsqrt(square / D + epsilon)
        for p, ref in enumerate(parts):
            gain = gain_ref[pl.ds(order_ref[p], 1), :]
            x_ref[p] = (ref[...].astype(F32) * inverse * gain).astype(BF16)
        acc_ref[...] = jnp.zeros_like(acc_ref)

    span = TP_WIDTH // 16

    def block(p, kind):
        start = order_ref[p] * span
        value = w_ref[pl.ds(start, span), pl.ds(kind * 16, 16), :]
        return value.reshape(TP_WIDTH, UNIT_BLOCK)

    gate = jnp.zeros((ROWS, UNIT_BLOCK), F32)
    up = jnp.zeros((ROWS, UNIT_BLOCK), F32)
    for p in range(4):
        gate += jnp.dot(x_ref[p], block(p, 0), preferred_element_type=F32)
        up += jnp.dot(x_ref[p], block(p, 1), preferred_element_type=F32)
    hidden = (gate / (1.0 + jnp.exp(-gate)) * up).astype(BF16)
    for p in range(4):
        acc_ref[p] += lax.dot_general(
            hidden, block(p, 2), (((1,), (1,)), ((), ())), preferred_element_type=F32
        )

    @pl.when(step == pl.num_programs(0) - 1)
    def _():
        out_ref[...] = acc_ref[...].astype(BF16)


def feed_forward(order, parts, gain, weights):
    whole = pl.BlockSpec((ROWS, TP_WIDTH), lambda i, o: (0, 0))
    units = weights.shape[2]
    return pl.pallas_call(
        feed_forward_kernel,
        out_shape=jax.ShapeDtypeStruct((4, ROWS, TP_WIDTH), BF16),
        grid_spec=pltpu.PrefetchScalarGridSpec(
            num_scalar_prefetch=1,
            grid=(units // UNIT_BLOCK,),
            in_specs=[whole] * 4
            + [
                pl.BlockSpec((4, TP_WIDTH), lambda i, o: (0, 0)),
                pl.BlockSpec((weights.shape[0], 48, UNIT_BLOCK), lambda i, o: (0, 0, i)),
            ],
            out_specs=pl.BlockSpec((4, ROWS, TP_WIDTH), lambda i, o: (0, 0, 0)),
            scratch_shapes=[
                pltpu.VMEM((4, ROWS, TP_WIDTH), BF16),
                pltpu.VMEM((4, ROWS, TP_WIDTH), F32),
            ],
        ),
        compiler_params=pltpu.CompilerParams(vmem_limit_bytes=40 << 20),
        cost_estimate=pl.CostEstimate(
            flops=6 * ROWS * D * units, bytes_accessed=14 << 20, transcendentals=ROWS * units
        ),
        name="feed_forward",
    )(order, *parts, gain, weights)


def on_device(
    residual_in,
    query_rows,
    key_rows,
    value_rows,
    lengths,
    norm_gain,
    gate_weight,
    up_weight,
    down_weight,
):
    packed = jnp.concatenate([gate_weight, up_weight, down_weight.T], axis=0)
    near = lax.all_gather(packed, "yh", axis=0, tiled=True)
    weights = lax.all_gather(near, ("x", "z"), axis=0, tiled=True).reshape(128, 48, -1)

    k1, v1 = from_behind(key_rows, 1), from_behind(value_rows, 1)
    lengths1, lengths2 = from_behind(lengths, 1), from_behind(lengths, 2)
    k2, v2 = from_behind(k1, 1), from_behind(v1, 1)
    gain = lax.all_gather(norm_gain, TP, axis=0)

    attended, sent = attention(
        jnp.concatenate([lengths, lengths1, lengths2]),
        query_rows, key_rows, value_rows, k1, v1, k2, v2, residual_in,
    )

    other_chip = swap(sent, "yl")
    other_core = swap(sent, "c")
    diagonal = swap(other_chip, "c")
    own = 2 * lax.axis_index("yl") + lax.axis_index("c")
    order = jnp.stack([own, own ^ 1, own ^ 2, own ^ 3]).astype(jnp.int32)
    partial = feed_forward(order, (sent, other_core, other_chip, diagonal), gain, weights)

    far = partial[2].astype(F32) + swap(partial[3], "c").astype(F32)
    close = partial[0].astype(F32) + swap(partial[1], "c").astype(F32)
    summed = close + swap(far.astype(BF16), "yl").astype(F32)
    mixed = residual_in + attended.astype(F32) + summed
    return attended, mixed


def solution(mesh):
    fine = Mesh(mesh.devices.reshape(4, 8, 4, 2, 2), SEQ + TP)
    placed = (
        P(SEQ, TP),
        P(SEQ, TP),
        P(SEQ, TP),
        P(SEQ, TP),
        P(SEQ),
        P(TP),
        P(SEQ, TP),
        P(SEQ, TP),
        P(TP, SEQ),
    )
    return jax.shard_map(
        on_device,
        mesh=fine,
        in_specs=placed,
        out_specs=(P(SEQ, TP), P(SEQ, TP)),
        check_vma=False,
    )
```

```python
import math

import jax
import jax.numpy as jnp
from jax import lax
from jax.experimental import pallas as pl
from jax.experimental.pallas import tpu as pltpu
from jax.sharding import Mesh
from jax.sharding import PartitionSpec as P

D = 2048
HEAD_DIM = 128
SEG = 128
ROWS = 256
TP_WIDTH = 512
UNIT_BLOCK = 256
epsilon = 1e-06

SEQ = ("x", "z", "yh")
TP = ("yl", "c")
F32 = jnp.float32
BF16 = jnp.bfloat16


def from_behind(value, by):
    size = lax.axis_size(SEQ)
    return lax.ppermute(value, SEQ, [(i, i + by) for i in range(size - by)])


def around(value, axis, by):
    size = lax.axis_size(axis)
    return lax.ppermute(value, axis, [(i, (i + by) % size) for i in range(size)])


def swap(value, axis):
    return lax.ppermute(value, axis, [(0, 1), (1, 0)])


def swap_x(value):
    return lax.ppermute(value, "x", [(i, i ^ 1) for i in range(4)])


def attention_kernel(
    lengths_ref, q_ref, k0_ref, v0_ref, k1_ref, v1_ref, k2_ref, v2_ref, res_ref, att_ref, send_ref
):
    rows = lax.broadcasted_iota(jnp.int32, (ROWS, ROWS), 0)
    cols = lax.broadcasted_iota(jnp.int32, (ROWS, ROWS), 1)
    col = lax.broadcasted_iota(jnp.int32, (1, ROWS), 1)

    def valid(key_ref):
        first = key_ref[pl.ds(ROWS, 8), pl.ds(0, ROWS)].astype(F32)[0:1, :].astype(jnp.int32)
        second = key_ref[pl.ds(ROWS + 8, 8), pl.ds(0, ROWS)].astype(F32)[0:1, :].astype(jnp.int32)
        return (col < jnp.where(col < SEG, first, second + SEG)).astype(jnp.int32)

    allowed = (
        (valid(k0_ref) > 0) & (cols <= rows),
        (valid(k1_ref) + jnp.zeros_like(cols)) > 0,
        (valid(k2_ref) > 0) & (cols > rows),
    )
    row = lax.broadcasted_iota(jnp.int32, (ROWS, 1), 0)
    keep = row < jnp.where(row < SEG, lengths_ref[0], lengths_ref[1] + SEG)
    scale = 1.0 / math.sqrt(HEAD_DIM)
    keys = (k0_ref, k1_ref, k2_ref)
    values = (v0_ref, v1_ref, v2_ref)
    for head in range(TP_WIDTH // HEAD_DIM):
        at = pl.ds(head * HEAD_DIM, HEAD_DIM)
        query = q_ref[:, at]
        masked = []
        for key_ref, allow in zip(keys, allowed):
            scores = lax.dot_general(
                query,
                key_ref[pl.ds(0, ROWS), at],
                (((1,), (1,)), ((), ())),
                preferred_element_type=F32,
            )
            masked.append(jnp.where(allow, scores * scale, -1e30))
        top = jnp.max(jnp.maximum(jnp.maximum(masked[0], masked[1]), masked[2]), axis=1, keepdims=True)
        weights = [jnp.where(a, jnp.exp(m - top), 0.0) for a, m in zip(allowed, masked)]
        denominator = jnp.sum(weights[0] + weights[1] + weights[2], axis=1, keepdims=True)
        numerator = jnp.zeros((ROWS, HEAD_DIM), F32)
        for weight, value_ref in zip(weights, values):
            numerator += jnp.dot(weight.astype(BF16), value_ref[:, at], preferred_element_type=F32)
        out = jnp.where(keep, numerator / jnp.where(keep, denominator, 1.0), 0.0).astype(BF16)
        att_ref[:, at] = out
        send_ref[:, at] = (res_ref[:, at] + out.astype(F32)).astype(BF16)


def attention(lengths, q, k0, v0, k1, v1, k2, v2, residual_in):
    shape = jax.ShapeDtypeStruct(q.shape, BF16)
    return pl.pallas_call(
        attention_kernel,
        out_shape=(shape, shape),
        in_specs=[pl.BlockSpec(memory_space=pltpu.SMEM)] + [pl.BlockSpec()] * 8,
        out_specs=(pl.BlockSpec(), pl.BlockSpec()),
        compiler_params=pltpu.CompilerParams(vmem_limit_bytes=32 << 20),
        cost_estimate=pl.CostEstimate(
            flops=4 * ROWS * 3 * ROWS * TP_WIDTH, bytes_accessed=3 << 20, transcendentals=3 << 18
        ),
        name="attention",
    )(lengths, q, k0, v0, k1, v1, k2, v2, residual_in)


def feed_forward_kernel(place_ref, *refs):
    parts, gain_ref, w_ref, outs, x_ref, acc_ref = (
        refs[:8], refs[8], refs[9], refs[10:18], refs[18], refs[19],
    )
    step = pl.program_id(0)

    @pl.when(step == 0)
    def _():
        for g in range(2):
            square = jnp.zeros((ROWS, 1), F32)
            for p in range(4):
                value = parts[4 * g + p][...].astype(F32)
                square += jnp.sum(value * value, axis=1, keepdims=True)
            inverse = lax.rsqrt(square / D + epsilon)
            for p in range(4):
                gain = gain_ref[pl.ds(place_ref[p], 1), :]
                value = parts[4 * g + p][...].astype(F32)
                x_ref[p, pl.ds(g * ROWS, ROWS), :] = (value * inverse * gain).astype(BF16)
        acc_ref[...] = jnp.zeros_like(acc_ref)

    def block(p, kind):
        pieces = [
            w_ref[:, pl.ds(place_ref[4 + p], 1), pl.ds(place_ref[8 + y], 1), pl.ds(kind * 16, 16), :]
            for y in range(4)
        ]
        return jnp.concatenate(pieces, axis=2).reshape(TP_WIDTH, UNIT_BLOCK)

    gate = jnp.zeros((2 * ROWS, UNIT_BLOCK), F32)
    up = jnp.zeros((2 * ROWS, UNIT_BLOCK), F32)
    for p in range(4):
        gate += jnp.dot(x_ref[p], block(p, 0), preferred_element_type=F32)
        up += jnp.dot(x_ref[p], block(p, 1), preferred_element_type=F32)
    hidden = (gate / (1.0 + jnp.exp(-gate)) * up).astype(BF16)
    for p in range(4):
        acc_ref[p] += lax.dot_general(
            hidden, block(p, 2), (((1,), (1,)), ((), ())), preferred_element_type=F32
        )

    @pl.when(step == pl.num_programs(0) - 1)
    def _():
        for g in range(2):
            for p in range(4):
                outs[4 * g + p][...] = acc_ref[p, pl.ds(g * ROWS, ROWS), :].astype(BF16)


def feed_forward(place, parts, gain, weights):
    whole = pl.BlockSpec((ROWS, TP_WIDTH), lambda i, o: (0, 0))
    units = weights.shape[4]
    return pl.pallas_call(
        feed_forward_kernel,
        out_shape=[jax.ShapeDtypeStruct((ROWS, TP_WIDTH), BF16)] * 8,
        grid_spec=pltpu.PrefetchScalarGridSpec(
            num_scalar_prefetch=1,
            grid=(units // UNIT_BLOCK,),
            in_specs=[whole] * 8
            + [
                pl.BlockSpec((4, TP_WIDTH), lambda i, o: (0, 0)),
                pl.BlockSpec((8, 4, 4, 48, UNIT_BLOCK), lambda i, o: (0, 0, 0, 0, i)),
            ],
            out_specs=[whole] * 8,
            scratch_shapes=[
                pltpu.VMEM((4, 2 * ROWS, TP_WIDTH), BF16),
                pltpu.VMEM((4, 2 * ROWS, TP_WIDTH), F32),
            ],
        ),
        compiler_params=pltpu.CompilerParams(vmem_limit_bytes=48 << 20),
        cost_estimate=pl.CostEstimate(
            flops=12 * ROWS * D * units, bytes_accessed=10 << 20, transcendentals=2 * ROWS * units
        ),
        name="feed_forward",
    )(place, *parts, gain, weights)


def on_device(
    residual_in,
    query_rows,
    key_rows,
    value_rows,
    lengths,
    norm_gain,
    gate_weight,
    up_weight,
    down_weight,
):
    x, yh = lax.axis_index("x"), lax.axis_index("yh")
    half = gate_weight.shape[1] // 2

    packed = jnp.concatenate([gate_weight, up_weight, down_weight.T], axis=0)
    near = [packed] + [around(packed, "yh", by) for by in (1, 2, 3)]
    parity = x & 1
    mine = jnp.stack([lax.dynamic_slice_in_dim(w, parity * half, half, 1) for w in near])
    other = jnp.stack([lax.dynamic_slice_in_dim(w, (1 - parity) * half, half, 1) for w in near])
    plane = jnp.stack([mine, around(other, "x", 1), around(mine, "x", 2), around(other, "x", 3)])
    weights = lax.all_gather(plane, "z", axis=0)

    tail = jnp.broadcast_to(
        jnp.repeat(lengths.astype(BF16), 8)[:, None], (16, key_rows.shape[1])
    )
    k0 = jnp.concatenate([key_rows, tail], axis=0)
    k1, v1 = from_behind(k0, 1), from_behind(value_rows, 1)
    k2, v2 = from_behind(k1, 1), from_behind(v1, 1)
    gain = lax.all_gather(norm_gain, TP, axis=0)
    residual_in, gain = lax.optimization_barrier((residual_in, gain))

    attended, sent = attention(
        lengths, query_rows, k0, value_rows, k1, v1, k2, v2, residual_in
    )

    partner = swap_x(sent)
    parts = []
    for start in (sent, partner):
        chip = swap(start, "yl")
        parts += [start, swap(start, "c"), chip, swap(chip, "c")]
    own = 2 * lax.axis_index("yl") + lax.axis_index("c")
    order = [own, own ^ 1, own ^ 2, own ^ 3]
    place = order + [(x - t) & 3 for t in order] + [(yh - y) & 3 for y in range(4)]
    outs = feed_forward(jnp.stack(place).astype(jnp.int32), parts, gain, weights)

    def add(left, right):
        return left.astype(F32) + right.astype(F32)

    def cores(g, p):
        return add(outs[4 * g + p], swap(outs[4 * g + p + 1], "c"))

    far = cores(0, 2) + swap_x(cores(1, 2).astype(BF16)).astype(F32)
    close = cores(0, 0) + swap_x(cores(1, 0).astype(BF16)).astype(F32)
    summed = close + swap(far.astype(BF16), "yl").astype(F32)
    mixed = residual_in + attended.astype(F32) + summed
    return attended, mixed


def solution(mesh):
    fine = Mesh(mesh.devices.reshape(4, 8, 4, 2, 2), SEQ + TP)
    placed = (
        P(SEQ, TP),
        P(SEQ, TP),
        P(SEQ, TP),
        P(SEQ, TP),
        P(SEQ),
        P(TP),
        P(SEQ, TP),
        P(SEQ, TP),
        P(TP, SEQ),
    )
    return jax.shard_map(
        on_device,
        mesh=fine,
        in_specs=placed,
        out_specs=(P(SEQ, TP), P(SEQ, TP)),
        check_vma=False,
    )
```

```python
import math

import jax
import jax.numpy as jnp
from jax import lax
from jax.experimental import pallas as pl
from jax.experimental.pallas import tpu as pltpu
from jax.sharding import Mesh
from jax.sharding import PartitionSpec as P

D = 2048
HEAD_DIM = 128
SEG = 128
ROWS = 256
TP_WIDTH = 512
UNIT_BLOCK = 256
UNITS = 512
EXTRA = 16
epsilon = 1e-06

SEQ = ("x", "z", "yh")
TP = ("yl", "c")
F32 = jnp.float32
BF16 = jnp.bfloat16


def from_behind(value, by):
    size = lax.axis_size(SEQ)
    return lax.ppermute(value, SEQ, [(i, i + by) for i in range(size - by)])


def around(value, axis, by):
    size = lax.axis_size(axis)
    return lax.ppermute(value, axis, [(i, (i + by) % size) for i in range(size)])


def swap(value, axis):
    return lax.ppermute(value, axis, [(0, 1), (1, 0)])


def attention_kernel(
    lengths_ref, gain_ref, *refs
):
    outside, (att_ref, send_ref), inside, sems = refs[:8], refs[8:10], refs[10:18], refs[18]
    copies = [
        pltpu.make_async_copy(src, dst, sems.at[i])
        for i, (src, dst) in enumerate(zip(outside, inside))
    ]
    for copy in copies:
        copy.start()
    q_ref, k0_ref, v0_ref, k1_ref, v1_ref, k2_ref, v2_ref, res_ref = inside
    gain = gain_ref[...]
    high = gain.astype(BF16).astype(F32)
    middle = (gain - high).astype(BF16).astype(F32)
    low = gain - high - middle
    extra = lax.broadcasted_iota(jnp.int32, (EXTRA, TP_WIDTH), 0)
    extra = jnp.where(extra == 0, high, jnp.where(extra == 1, middle, jnp.where(extra == 2, low, 0.0)))
    send_ref[pl.ds(ROWS, EXTRA), :] = extra.astype(BF16)
    for copy in copies:
        copy.wait()
    rows = lax.broadcasted_iota(jnp.int32, (ROWS, ROWS), 0)
    cols = lax.broadcasted_iota(jnp.int32, (ROWS, ROWS), 1)
    col = lax.broadcasted_iota(jnp.int32, (1, ROWS), 1)

    def valid(key_ref):
        first = key_ref[pl.ds(ROWS, 8), pl.ds(0, ROWS)].astype(F32)[0:1, :].astype(jnp.int32)
        second = key_ref[pl.ds(ROWS + 8, 8), pl.ds(0, ROWS)].astype(F32)[0:1, :].astype(jnp.int32)
        return (col < jnp.where(col < SEG, first, second + SEG)).astype(jnp.int32)

    allowed = (
        (valid(k0_ref) > 0) & (cols <= rows),
        (valid(k1_ref) + jnp.zeros_like(cols)) > 0,
        (valid(k2_ref) > 0) & (cols > rows),
    )
    row = lax.broadcasted_iota(jnp.int32, (ROWS, 1), 0)
    keep = row < jnp.where(row < SEG, lengths_ref[0], lengths_ref[1] + SEG)
    scale = 1.0 / math.sqrt(HEAD_DIM)
    keys = (k0_ref, k1_ref, k2_ref)
    values = (v0_ref, v1_ref, v2_ref)
    for head in range(TP_WIDTH // HEAD_DIM):
        at = pl.ds(head * HEAD_DIM, HEAD_DIM)
        query = q_ref[:, at]
        masked = []
        for key_ref, allow in zip(keys, allowed):
            scores = lax.dot_general(
                query,
                key_ref[pl.ds(0, ROWS), at],
                (((1,), (1,)), ((), ())),
                preferred_element_type=F32,
            )
            masked.append(jnp.where(allow, scores * scale, -1e30))
        top = jnp.max(jnp.maximum(jnp.maximum(masked[0], masked[1]), masked[2]), axis=1, keepdims=True)
        weights = [jnp.where(a, jnp.exp(m - top), 0.0) for a, m in zip(allowed, masked)]
        denominator = jnp.sum(weights[0] + weights[1] + weights[2], axis=1, keepdims=True)
        numerator = jnp.zeros((ROWS, HEAD_DIM), F32)
        for weight, value_ref in zip(weights, values):
            numerator += jnp.dot(weight.astype(BF16), value_ref[:, at], preferred_element_type=F32)
        out = jnp.where(keep, numerator / jnp.where(keep, denominator, 1.0), 0.0).astype(BF16)
        att_ref[:, at] = out
        send_ref[pl.ds(0, ROWS), at] = (res_ref[:, at] + out.astype(F32)).astype(BF16)


def attention(lengths, gain, q, k0, v0, k1, v1, k2, v2, residual_in):
    return pl.pallas_call(
        attention_kernel,
        out_shape=(
            jax.ShapeDtypeStruct((ROWS, TP_WIDTH), BF16),
            jax.ShapeDtypeStruct((ROWS + EXTRA, TP_WIDTH), BF16),
        ),
        in_specs=[SMEM, pl.BlockSpec()] + [HBM] * 8,
        out_specs=(pl.BlockSpec(), pl.BlockSpec()),
        scratch_shapes=[
            pltpu.VMEM(a.shape, a.dtype) for a in (q, k0, v0, k1, v1, k2, v2, residual_in)
        ]
        + [pltpu.SemaphoreType.DMA((8,))],
        compiler_params=pltpu.CompilerParams(vmem_limit_bytes=60 << 20),
        cost_estimate=pl.CostEstimate(
            flops=4 * ROWS * 3 * ROWS * TP_WIDTH, bytes_accessed=3 << 20, transcendentals=3 << 18
        ),
        name="attention",
    )(lengths, gain, q, k0, v0, k1, v1, k2, v2, residual_in)


def through_units(x_ref, acc_ref, load):
    for low in range(0, UNITS, UNIT_BLOCK):
        gate = jnp.zeros((ROWS, UNIT_BLOCK), F32)
        up = jnp.zeros((ROWS, UNIT_BLOCK), F32)
        for p in range(4):
            gate += jnp.dot(x_ref[p], load(p, 0, low), preferred_element_type=F32)
            up += jnp.dot(x_ref[p], load(p, 1, low), preferred_element_type=F32)
        hidden = (gate / (1.0 + jnp.exp(-gate)) * up).astype(BF16)
        for p in range(4):
            acc_ref[p] += lax.dot_general(
                hidden, load(p, 2, low), (((1,), (1,)), ((), ())), preferred_element_type=F32
            )


def first_units_kernel(place_ref, *refs):
    parts, blocks, halves = refs[:4], refs[4:11], refs[11:13]
    x_ref, acc_ref, w_ref, sems = refs[13:]
    copies = [
        pltpu.make_async_copy(block, w_ref.at[place_ref[12 + i]], sems.at[i])
        for i, block in enumerate(blocks)
    ] + [
        pltpu.make_async_copy(half, w_ref.at[place_ref[19], pl.ds(2 * i, 2)], sems.at[7 + i])
        for i, half in enumerate(halves)
    ]
    for copy in copies:
        copy.start()
    square = jnp.zeros((ROWS, 1), F32)
    for ref in parts:
        value = ref[pl.ds(0, ROWS), :].astype(F32)
        square += jnp.sum(value * value, axis=1, keepdims=True)
    inverse = lax.rsqrt(square / D + epsilon)
    for p, ref in enumerate(parts):
        extra = ref[pl.ds(ROWS, EXTRA), :].astype(F32)
        gain = extra[0:1] + extra[1:2] + extra[2:3]
        x_ref[p] = (ref[pl.ds(0, ROWS), :].astype(F32) * inverse * gain).astype(BF16)
    acc_ref[...] = jnp.zeros_like(acc_ref)
    for copy in copies:
        copy.wait()

    def load(p, kind, low):
        pieces = [
            w_ref[
                :,
                pl.ds(place_ref[4 + p], 1),
                pl.ds(place_ref[8 + y], 1),
                pl.ds(kind * 16, 16),
                pl.ds(low, UNIT_BLOCK),
            ]
            for y in range(4)
        ]
        return jnp.concatenate(pieces, axis=2).reshape(TP_WIDTH, UNIT_BLOCK)

    through_units(x_ref, acc_ref, load)


def last_units_kernel(place_ref, x_ref, acc_in, *refs):
    blocks, halves, outs, acc_ref, w_ref, sems = (
        refs[:3], refs[3:5], refs[5:9], refs[9], refs[10], refs[11],
    )
    copies = [
        pltpu.make_async_copy(block, w_ref.at[place_ref[20 + i]], sems.at[i])
        for i, block in enumerate(blocks)
    ] + [
        pltpu.make_async_copy(half, w_ref.at[place_ref[23], pl.ds(4 * i, 4)], sems.at[3 + i])
        for i, half in enumerate(halves)
    ]
    for copy in copies:
        copy.start()
    acc_ref[...] = acc_in[...]
    for copy in copies:
        copy.wait()

    def load(p, kind, low):
        pieces = [
            w_ref[
                pl.ds(place_ref[p], 1),
                :,
                pl.ds(place_ref[8 + y], 1),
                pl.ds(kind * 16, 16),
                pl.ds(low, UNIT_BLOCK),
            ]
            for y in range(4)
        ]
        return jnp.concatenate(pieces, axis=2).reshape(TP_WIDTH, UNIT_BLOCK)

    through_units(x_ref, acc_ref, load)
    for p in range(4):
        outs[p][...] = acc_ref[p].astype(BF16)


HBM = pl.BlockSpec(memory_space=pltpu.HBM)
SMEM = pl.BlockSpec(memory_space=pltpu.SMEM)


def units_cost():
    return pl.CostEstimate(
        flops=6 * ROWS * D * UNITS, bytes_accessed=10 << 20, transcendentals=ROWS * UNITS
    )


def first_units(place, parts, blocks, halves):
    return pl.pallas_call(
        first_units_kernel,
        out_shape=(
            jax.ShapeDtypeStruct((4, ROWS, TP_WIDTH), BF16),
            jax.ShapeDtypeStruct((4, ROWS, TP_WIDTH), F32),
        ),
        in_specs=[SMEM] + [pl.BlockSpec()] * 4 + [HBM] * 9,
        out_specs=(pl.BlockSpec(), pl.BlockSpec()),
        scratch_shapes=[pltpu.VMEM((8, 4, 4, 48, UNITS), BF16), pltpu.SemaphoreType.DMA((9,))],
        compiler_params=pltpu.CompilerParams(vmem_limit_bytes=60 << 20),
        cost_estimate=units_cost(),
        name="first_units",
    )(place, *parts, *blocks, *halves)


def last_units(place, x, acc, blocks, halves):
    return pl.pallas_call(
        last_units_kernel,
        out_shape=[jax.ShapeDtypeStruct((ROWS, TP_WIDTH), BF16)] * 4,
        in_specs=[SMEM] + [pl.BlockSpec()] * 2 + [HBM] * 5,
        out_specs=[pl.BlockSpec()] * 4,
        scratch_shapes=[
            pltpu.VMEM((4, ROWS, TP_WIDTH), F32),
            pltpu.VMEM((4, 8, 4, 48, UNITS), BF16),
            pltpu.SemaphoreType.DMA((5,)),
        ],
        compiler_params=pltpu.CompilerParams(vmem_limit_bytes=60 << 20),
        cost_estimate=units_cost(),
        name="last_units",
    )(place, x, acc, *blocks, *halves)


def on_device(
    residual_in,
    query_rows,
    key_rows,
    value_rows,
    lengths,
    norm_gain,
    gate_weight,
    up_weight,
    down_weight,
):
    x, z, yh = (lax.axis_index(axis) for axis in SEQ)

    packed = jnp.concatenate([gate_weight, up_weight, down_weight.T], axis=0)
    near = [packed] + [around(packed, "yh", by) for by in (1, 2, 3)]
    first = jnp.stack([w[:, :UNITS] for w in near])
    second = jnp.stack([w[:, UNITS:] for w in near])
    line = lax.all_gather(second, "z", axis=0)
    plane = jnp.stack([first] + [around(first, "x", by) for by in (1, 2, 3)])

    tail = jnp.broadcast_to(
        jnp.repeat(lengths.astype(BF16), 8)[:, None], (16, key_rows.shape[1])
    )
    k0 = jnp.concatenate([key_rows, tail], axis=0)
    k1, v1 = from_behind(k0, 1), from_behind(value_rows, 1)

    plane, k1, v1 = lax.optimization_barrier((plane, k1, v1))
    k2, v2 = from_behind(k1, 1), from_behind(v1, 1)
    line, k2, v2 = lax.optimization_barrier((line, k2, v2))

    attended, sent = attention(
        lengths, norm_gain[None, :], query_rows, k0, value_rows, k1, v1, k2, v2, residual_in
    )

    forward, backward = [plane], [plane]
    for by in range(3):
        if by == 2:
            forward[2], backward[2], sent = lax.optimization_barrier((forward[2], backward[2], sent))
        forward.append(around(forward[-1], "z", 1))
        backward.append(around(backward[-1], "z", -1))
    z_blocks = forward + backward[1:]
    z_halves = [around(forward[3][:2], "z", 1), around(backward[3][2:], "z", -1)]
    z_place = [z, z - 1, z - 2, z - 3, z + 1, z + 2, z + 3, z + 4]

    x_blocks = [line, around(line, "x", 1), around(line, "x", -1)]
    x_halves = [around(x_blocks[1][:4], "x", 1), around(x_blocks[2][4:], "x", -1)]
    x_place = [x, x - 1, x + 1, x + 2]

    chip = swap(sent, "yl")
    parts = [sent, swap(sent, "c"), chip, swap(chip, "c")]
    own = 2 * lax.axis_index("yl") + lax.axis_index("c")
    order = [own, own ^ 1, own ^ 2, own ^ 3]
    place = (
        order
        + [(x - t) & 3 for t in order]
        + [(yh - y) & 3 for y in range(4)]
        + [at & 7 for at in z_place]
        + [at & 3 for at in x_place]
    )
    place = jnp.stack(place).astype(jnp.int32)
    normed, acc = first_units(place, parts, z_blocks, z_halves)
    outs = last_units(place, normed, acc, x_blocks, x_halves)

    def add(left, right):
        return left.astype(F32) + right.astype(F32)

    far = add(outs[2], swap(outs[3], "c"))
    close = add(outs[0], swap(outs[1], "c"))
    summed = close + swap(far.astype(BF16), "yl").astype(F32)
    mixed = residual_in + attended.astype(F32) + summed
    return attended, mixed


def solution(mesh):
    fine = Mesh(mesh.devices.reshape(4, 8, 4, 2, 2), SEQ + TP)
    placed = (
        P(SEQ, TP),
        P(SEQ, TP),
        P(SEQ, TP),
        P(SEQ, TP),
        P(SEQ),
        P(TP),
        P(SEQ, TP),
        P(SEQ, TP),
        P(TP, SEQ),
    )
    return jax.shard_map(
        on_device,
        mesh=fine,
        in_specs=placed,
        out_specs=(P(SEQ, TP), P(SEQ, TP)),
        check_vma=False,
    )
```

```python
import math

import jax
import jax.numpy as jnp
from jax import lax
from jax.experimental import pallas as pl
from jax.experimental.pallas import tpu as pltpu
from jax.sharding import Mesh
from jax.sharding import PartitionSpec as P

D = 2048
HEAD_DIM = 128
SEG = 128
ROWS = 256
TP_WIDTH = 512
UNIT_BLOCK = 256
EXTRA = 16
epsilon = 1e-06

SEQ = ("x", "z", "yh")
TP = ("yl", "c")
F32 = jnp.float32
BF16 = jnp.bfloat16


def from_behind(value, by):
    size = lax.axis_size(SEQ)
    return lax.ppermute(value, SEQ, [(i, i + by) for i in range(size - by)])


def around(value, axis, by):
    size = lax.axis_size(axis)
    return lax.ppermute(value, axis, [(i, (i + by) % size) for i in range(size)])


def swap(value, axis):
    size = lax.axis_size(axis)
    return lax.ppermute(value, axis, [(i, i ^ 1) for i in range(size)])


def attention_kernel(
    lengths_ref, gain_ref, *refs
):
    outside, (att_ref, send_ref), inside, sems = refs[:8], refs[8:10], refs[10:18], refs[18]
    copies = [
        pltpu.make_async_copy(src, dst, sems.at[i])
        for i, (src, dst) in enumerate(zip(outside, inside))
    ]
    for copy in copies:
        copy.start()
    q_ref, k0_ref, v0_ref, k1_ref, v1_ref, k2_ref, v2_ref, res_ref = inside
    gain = gain_ref[...]
    high = gain.astype(BF16).astype(F32)
    middle = (gain - high).astype(BF16).astype(F32)
    low = gain - high - middle
    extra = lax.broadcasted_iota(jnp.int32, (EXTRA, TP_WIDTH), 0)
    extra = jnp.where(extra == 0, high, jnp.where(extra == 1, middle, jnp.where(extra == 2, low, 0.0)))
    send_ref[pl.ds(ROWS, EXTRA), :] = extra.astype(BF16)
    for copy in copies:
        copy.wait()
    rows = lax.broadcasted_iota(jnp.int32, (ROWS, ROWS), 0)
    cols = lax.broadcasted_iota(jnp.int32, (ROWS, ROWS), 1)
    col = lax.broadcasted_iota(jnp.int32, (1, ROWS), 1)

    def valid(key_ref):
        first = key_ref[pl.ds(ROWS, 8), pl.ds(0, ROWS)].astype(F32)[0:1, :].astype(jnp.int32)
        second = key_ref[pl.ds(ROWS + 8, 8), pl.ds(0, ROWS)].astype(F32)[0:1, :].astype(jnp.int32)
        return (col < jnp.where(col < SEG, first, second + SEG)).astype(jnp.int32)

    allowed = (
        (valid(k0_ref) > 0) & (cols <= rows),
        (valid(k1_ref) + jnp.zeros_like(cols)) > 0,
        (valid(k2_ref) > 0) & (cols > rows),
    )
    row = lax.broadcasted_iota(jnp.int32, (ROWS, 1), 0)
    keep = row < jnp.where(row < SEG, lengths_ref[0], lengths_ref[1] + SEG)
    scale = 1.0 / math.sqrt(HEAD_DIM)
    keys = (k0_ref, k1_ref, k2_ref)
    values = (v0_ref, v1_ref, v2_ref)
    for head in range(TP_WIDTH // HEAD_DIM):
        at = pl.ds(head * HEAD_DIM, HEAD_DIM)
        query = q_ref[:, at]
        masked = []
        for key_ref, allow in zip(keys, allowed):
            scores = lax.dot_general(
                query,
                key_ref[pl.ds(0, ROWS), at],
                (((1,), (1,)), ((), ())),
                preferred_element_type=F32,
            )
            masked.append(jnp.where(allow, scores * scale, -1e30))
        top = jnp.max(jnp.maximum(jnp.maximum(masked[0], masked[1]), masked[2]), axis=1, keepdims=True)
        weights = [jnp.where(a, jnp.exp(m - top), 0.0) for a, m in zip(allowed, masked)]
        denominator = jnp.sum(weights[0] + weights[1] + weights[2], axis=1, keepdims=True)
        numerator = jnp.zeros((ROWS, HEAD_DIM), F32)
        for weight, value_ref in zip(weights, values):
            numerator += jnp.dot(weight.astype(BF16), value_ref[:, at], preferred_element_type=F32)
        out = jnp.where(keep, numerator / jnp.where(keep, denominator, 1.0), 0.0).astype(BF16)
        att_ref[:, at] = out
        send_ref[pl.ds(0, ROWS), at] = (res_ref[:, at] + out.astype(F32)).astype(BF16)


HBM = pl.BlockSpec(memory_space=pltpu.HBM)
SMEM = pl.BlockSpec(memory_space=pltpu.SMEM)


def attention(lengths, gain, q, k0, v0, k1, v1, k2, v2, residual_in):
    return pl.pallas_call(
        attention_kernel,
        out_shape=(
            jax.ShapeDtypeStruct((ROWS, TP_WIDTH), BF16),
            jax.ShapeDtypeStruct((ROWS + EXTRA, TP_WIDTH), BF16),
        ),
        in_specs=[SMEM, pl.BlockSpec()] + [HBM] * 8,
        out_specs=(pl.BlockSpec(), pl.BlockSpec()),
        scratch_shapes=[
            pltpu.VMEM(a.shape, a.dtype) for a in (q, k0, v0, k1, v1, k2, v2, residual_in)
        ]
        + [pltpu.SemaphoreType.DMA((8,))],
        compiler_params=pltpu.CompilerParams(vmem_limit_bytes=60 << 20),
        cost_estimate=pl.CostEstimate(
            flops=4 * ROWS * 3 * ROWS * TP_WIDTH, bytes_accessed=3 << 20, transcendentals=3 << 18
        ),
        name="attention",
    )(lengths, gain, q, k0, v0, k1, v1, k2, v2, residual_in)


def feed_forward_kernel(place_ref, *refs):
    parts, w_ref, outs, x_ref, acc_ref = refs[:8], refs[8], refs[9:13], refs[13], refs[14]
    step = pl.program_id(0)

    @pl.when(step == 0)
    def _():
        for g in range(2):
            square = jnp.zeros((ROWS, 1), F32)
            for p in range(4):
                value = parts[4 * g + p][pl.ds(0, ROWS), :].astype(F32)
                square += jnp.sum(value * value, axis=1, keepdims=True)
            inverse = lax.rsqrt(square / D + epsilon)
            for p in range(4):
                extra = parts[4 * g + p][pl.ds(ROWS, EXTRA), :].astype(F32)
                gain = extra[0:1] + extra[1:2] + extra[2:3]
                value = parts[4 * g + p][pl.ds(0, ROWS), :].astype(F32)
                x_ref[p, pl.ds(g * ROWS, ROWS), :] = (value * inverse * gain).astype(BF16)
        acc_ref[...] = jnp.zeros_like(acc_ref)

    def block(p, kind):
        pieces = [
            w_ref[
                pl.ds(place_ref[p] * 8, 8),
                pl.ds(place_ref[4 + y], 1),
                pl.ds(kind * 16, 16),
                :,
            ]
            for y in range(4)
        ]
        return jnp.concatenate(pieces, axis=1).reshape(TP_WIDTH, UNIT_BLOCK)

    gate = jnp.zeros((2 * ROWS, UNIT_BLOCK), F32)
    up = jnp.zeros((2 * ROWS, UNIT_BLOCK), F32)
    for p in range(4):
        gate += jnp.dot(x_ref[p], block(p, 0), preferred_element_type=F32)
        up += jnp.dot(x_ref[p], block(p, 1), preferred_element_type=F32)
    hidden = (gate / (1.0 + jnp.exp(-gate)) * up).astype(BF16)
    for p in range(4):
        acc_ref[p] += lax.dot_general(
            hidden, block(p, 2), (((1,), (1,)), ((), ())), preferred_element_type=F32
        )

    @pl.when(step == pl.num_programs(0) - 1)
    def _():
        for g in range(2):
            for i, p in enumerate((2, 0)):
                outs[2 * g][i] = acc_ref[p, pl.ds(g * ROWS, ROWS), :].astype(BF16)
                outs[2 * g + 1][i] = acc_ref[p + 1, pl.ds(g * ROWS, ROWS), :].astype(BF16)


def feed_forward(place, parts, weights):
    whole = pl.BlockSpec((ROWS + EXTRA, TP_WIDTH), lambda i, o: (0, 0))
    pair = pl.BlockSpec((2, ROWS, TP_WIDTH), lambda i, o: (0, 0, 0))
    units = weights.shape[3]
    return pl.pallas_call(
        feed_forward_kernel,
        out_shape=[jax.ShapeDtypeStruct((2, ROWS, TP_WIDTH), BF16)] * 4,
        grid_spec=pltpu.PrefetchScalarGridSpec(
            num_scalar_prefetch=1,
            grid=(units // UNIT_BLOCK,),
            in_specs=[whole] * 8
            + [pl.BlockSpec((32, 4, 48, UNIT_BLOCK), lambda i, o: (0, 0, 0, i))],
            out_specs=[pair] * 4,
            scratch_shapes=[
                pltpu.VMEM((4, 2 * ROWS, TP_WIDTH), BF16),
                pltpu.VMEM((4, 2 * ROWS, TP_WIDTH), F32),
            ],
        ),
        compiler_params=pltpu.CompilerParams(vmem_limit_bytes=48 << 20),
        cost_estimate=pl.CostEstimate(
            flops=12 * ROWS * D * units, bytes_accessed=10 << 20, transcendentals=2 * ROWS * units
        ),
        name="feed_forward",
    )(place, *parts, weights)


def on_device(
    residual_in,
    query_rows,
    key_rows,
    value_rows,
    lengths,
    norm_gain,
    gate_weight,
    up_weight,
    down_weight,
):
    yh = lax.axis_index("yh")
    half = gate_weight.shape[1] // 2

    packed = jnp.concatenate([gate_weight, up_weight, down_weight.T], axis=0)
    parity = yh & 1
    mine = lax.dynamic_slice_in_dim(packed, parity * half, half, 1)
    other = lax.dynamic_slice_in_dim(packed, (1 - parity) * half, half, 1)
    near = jnp.stack(
        [mine, around(other, "yh", 1), around(mine, "yh", 2), around(other, "yh", 3)]
    )
    weights = lax.all_gather(near, ("x", "z"), axis=0)

    tail = jnp.broadcast_to(
        jnp.repeat(lengths.astype(BF16), 8)[:, None], (16, key_rows.shape[1])
    )
    k0 = jnp.concatenate([key_rows, tail], axis=0)
    k1, v1 = from_behind(k0, 1), from_behind(value_rows, 1)
    k2, v2 = from_behind(k1, 1), from_behind(v1, 1)

    attended, sent = attention(
        lengths, norm_gain[None, :], query_rows, k0, value_rows, k1, v1, k2, v2, residual_in
    )

    partner = swap(sent, "yh")
    parts = []
    for start in (sent, partner):
        chip = swap(start, "yl")
        parts += [start, swap(start, "c"), chip, swap(chip, "c")]
    own = 2 * lax.axis_index("yl") + lax.axis_index("c")
    place = [own, own ^ 1, own ^ 2, own ^ 3] + [(yh - y) & 3 for y in range(4)]
    place = jnp.stack(place).astype(jnp.int32)
    own_keep, own_send, partner_keep, partner_send = feed_forward(place, parts, weights)

    def add(left, right):
        return left.astype(F32) + right.astype(F32)

    partner_got = swap(partner_send, "c")
    own_got = swap(own_send, "c")
    partner_far = swap(add(partner_keep[0], partner_got[0]).astype(BF16), "yl")
    own_far = swap(add(own_keep[0], own_got[0]).astype(BF16), "yl")
    back = swap((add(partner_keep[1], partner_got[1]) + partner_far.astype(F32)).astype(BF16), "yh")
    summed = add(own_keep[1], own_got[1]) + own_far.astype(F32) + back.astype(F32)
    mixed = residual_in + attended.astype(F32) + summed
    return attended, mixed


def solution(mesh):
    fine = Mesh(mesh.devices.reshape(4, 8, 4, 2, 2), SEQ + TP)
    placed = (
        P(SEQ, TP),
        P(SEQ, TP),
        P(SEQ, TP),
        P(SEQ, TP),
        P(SEQ),
        P(TP),
        P(SEQ, TP),
        P(SEQ, TP),
        P(TP, SEQ),
    )
    return jax.shard_map(
        on_device,
        mesh=fine,
        in_specs=placed,
        out_specs=(P(SEQ, TP), P(SEQ, TP)),
        check_vma=False,
    )
```

```python
import math

import jax
import jax.numpy as jnp
from jax import lax
from jax.experimental import pallas as pl
from jax.experimental.pallas import tpu as pltpu
from jax.sharding import Mesh
from jax.sharding import PartitionSpec as P

D = 2048
HEAD_DIM = 128
SEG = 128
ROWS = 256
TP_WIDTH = 512
UNIT_BLOCK = 256
EXTRA = 16
epsilon = 1e-06

SEQ = ("x", "z", "yh")
TP = ("yl", "c")
F32 = jnp.float32
BF16 = jnp.bfloat16


def from_behind(value, by):
    size = lax.axis_size(SEQ)
    return lax.ppermute(value, SEQ, [(i, i + by) for i in range(size - by)])


def around(value, axis, by):
    size = lax.axis_size(axis)
    return lax.ppermute(value, axis, [(i, (i + by) % size) for i in range(size)])


def swap(value, axis):
    size = lax.axis_size(axis)
    return lax.ppermute(value, axis, [(i, i ^ 1) for i in range(size)])


def attention_kernel(
    lengths_ref, gain_ref, *refs
):
    outside, (att_ref, send_ref), inside, sems = refs[:8], refs[8:10], refs[10:18], refs[18]
    copies = [
        pltpu.make_async_copy(src, dst, sems.at[i])
        for i, (src, dst) in enumerate(zip(outside, inside))
    ]
    for copy in copies:
        copy.start()
    q_ref, k0_ref, v0_ref, k1_ref, v1_ref, k2_ref, v2_ref, res_ref = inside
    gain = gain_ref[...]
    high = gain.astype(BF16).astype(F32)
    middle = (gain - high).astype(BF16).astype(F32)
    low = gain - high - middle
    extra = lax.broadcasted_iota(jnp.int32, (EXTRA, TP_WIDTH), 0)
    extra = jnp.where(extra == 0, high, jnp.where(extra == 1, middle, jnp.where(extra == 2, low, 0.0)))
    send_ref[pl.ds(ROWS, EXTRA), :] = extra.astype(BF16)
    for copy in copies:
        copy.wait()
    rows = lax.broadcasted_iota(jnp.int32, (ROWS, ROWS), 0)
    cols = lax.broadcasted_iota(jnp.int32, (ROWS, ROWS), 1)
    col = lax.broadcasted_iota(jnp.int32, (1, ROWS), 1)

    def valid(key_ref):
        first = key_ref[pl.ds(ROWS, 8), pl.ds(0, ROWS)].astype(F32)[0:1, :].astype(jnp.int32)
        second = key_ref[pl.ds(ROWS + 8, 8), pl.ds(0, ROWS)].astype(F32)[0:1, :].astype(jnp.int32)
        return (col < jnp.where(col < SEG, first, second + SEG)).astype(jnp.int32)

    allowed = (
        (valid(k0_ref) > 0) & (cols <= rows),
        (valid(k1_ref) + jnp.zeros_like(cols)) > 0,
        (valid(k2_ref) > 0) & (cols > rows),
    )
    row = lax.broadcasted_iota(jnp.int32, (ROWS, 1), 0)
    keep = row < jnp.where(row < SEG, lengths_ref[0], lengths_ref[1] + SEG)
    scale = 1.0 / math.sqrt(HEAD_DIM)
    keys = (k0_ref, k1_ref, k2_ref)
    values = (v0_ref, v1_ref, v2_ref)
    for head in range(TP_WIDTH // HEAD_DIM):
        at = pl.ds(head * HEAD_DIM, HEAD_DIM)
        query = q_ref[:, at]
        masked = []
        for key_ref, allow in zip(keys, allowed):
            scores = lax.dot_general(
                query,
                key_ref[pl.ds(0, ROWS), at],
                (((1,), (1,)), ((), ())),
                preferred_element_type=F32,
            )
            masked.append(jnp.where(allow, scores * scale, -1e30))
        top = jnp.max(jnp.maximum(jnp.maximum(masked[0], masked[1]), masked[2]), axis=1, keepdims=True)
        weights = [jnp.where(a, jnp.exp(m - top), 0.0) for a, m in zip(allowed, masked)]
        denominator = jnp.sum(weights[0] + weights[1] + weights[2], axis=1, keepdims=True)
        numerator = jnp.zeros((ROWS, HEAD_DIM), F32)
        for weight, value_ref in zip(weights, values):
            numerator += jnp.dot(weight.astype(BF16), value_ref[:, at], preferred_element_type=F32)
        out = jnp.where(keep, numerator / jnp.where(keep, denominator, 1.0), 0.0).astype(BF16)
        att_ref[:, at] = out
        send_ref[pl.ds(0, ROWS), at] = (res_ref[:, at] + out.astype(F32)).astype(BF16)


HBM = pl.BlockSpec(memory_space=pltpu.HBM)
SMEM = pl.BlockSpec(memory_space=pltpu.SMEM)


def attention(lengths, gain, q, k0, v0, k1, v1, k2, v2, residual_in):
    return pl.pallas_call(
        attention_kernel,
        out_shape=(
            jax.ShapeDtypeStruct((ROWS, TP_WIDTH), BF16),
            jax.ShapeDtypeStruct((ROWS + EXTRA, TP_WIDTH), BF16),
        ),
        in_specs=[SMEM, pl.BlockSpec()] + [HBM] * 8,
        out_specs=(pl.BlockSpec(), pl.BlockSpec()),
        scratch_shapes=[
            pltpu.VMEM(a.shape, a.dtype) for a in (q, k0, v0, k1, v1, k2, v2, residual_in)
        ]
        + [pltpu.SemaphoreType.DMA((8,))],
        compiler_params=pltpu.CompilerParams(vmem_limit_bytes=60 << 20),
        cost_estimate=pl.CostEstimate(
            flops=4 * ROWS * 3 * ROWS * TP_WIDTH, bytes_accessed=3 << 20, transcendentals=3 << 18
        ),
        name="attention",
    )(lengths, gain, q, k0, v0, k1, v1, k2, v2, residual_in)


def normalize_kernel(*refs):
    parts, outs = refs[:8], refs[8:]
    for g in range(2):
        square = jnp.zeros((ROWS, 1), F32)
        for p in range(4):
            value = parts[4 * g + p][pl.ds(0, ROWS), :].astype(F32)
            square += jnp.sum(value * value, axis=1, keepdims=True)
        inverse = lax.rsqrt(square / D + epsilon)
        for p in range(4):
            extra = parts[4 * g + p][pl.ds(ROWS, EXTRA), :].astype(F32)
            gain = extra[0:1] + extra[1:2] + extra[2:3]
            value = parts[4 * g + p][pl.ds(0, ROWS), :].astype(F32)
            outs[g][p] = (value * inverse * gain).astype(BF16)


def normalize(parts):
    return pl.pallas_call(
        normalize_kernel,
        out_shape=[jax.ShapeDtypeStruct((4, ROWS, TP_WIDTH), BF16)] * 2,
        compiler_params=pltpu.CompilerParams(vmem_limit_bytes=32 << 20),
        cost_estimate=pl.CostEstimate(flops=8 * ROWS * D, bytes_accessed=4 << 20, transcendentals=0),
        name="normalize",
    )(*parts)


def feed_forward_kernel(place_ref, x_ref, w_ref, keep_ref, send_ref, acc_ref):
    step = pl.program_id(0)

    def block(p, kind):
        pieces = [
            w_ref[
                pl.ds(place_ref[p] * 8, 8),
                pl.ds(place_ref[4 + y], 1),
                pl.ds(kind * 16, 16),
                :,
            ]
            for y in range(4)
        ]
        return jnp.concatenate(pieces, axis=1).reshape(TP_WIDTH, UNIT_BLOCK)

    gate = jnp.zeros((ROWS, UNIT_BLOCK), F32)
    up = jnp.zeros((ROWS, UNIT_BLOCK), F32)
    for p in range(4):
        gate += jnp.dot(x_ref[p], block(p, 0), preferred_element_type=F32)
        up += jnp.dot(x_ref[p], block(p, 1), preferred_element_type=F32)
    hidden = (gate / (1.0 + jnp.exp(-gate)) * up).astype(BF16)

    def down(p):
        return lax.dot_general(
            hidden, block(p, 2), (((1,), (1,)), ((), ())), preferred_element_type=F32
        )

    @pl.when(step == 0)
    def _():
        for p in range(4):
            acc_ref[p] = down(p)

    @pl.when(step == 1)
    def _():
        for i, p in enumerate((2, 0)):
            send_ref[i] = (acc_ref[p + 1] + down(p + 1)).astype(BF16)
            keep_ref[i] = (acc_ref[p] + down(p)).astype(BF16)


def feed_forward(place, x, weights):
    pair = pl.BlockSpec((2, ROWS, TP_WIDTH), lambda i, o: (0, 0, 0))
    units = weights.shape[3]
    assert units == 2 * UNIT_BLOCK
    return pl.pallas_call(
        feed_forward_kernel,
        out_shape=[jax.ShapeDtypeStruct((2, ROWS, TP_WIDTH), BF16)] * 2,
        grid_spec=pltpu.PrefetchScalarGridSpec(
            num_scalar_prefetch=1,
            grid=(2,),
            in_specs=[
                pl.BlockSpec((4, ROWS, TP_WIDTH), lambda i, o: (0, 0, 0)),
                pl.BlockSpec((32, 4, 48, UNIT_BLOCK), lambda i, o: (0, 0, 0, i)),
            ],
            out_specs=[pair] * 2,
            scratch_shapes=[pltpu.VMEM((4, ROWS, TP_WIDTH), F32)],
        ),
        compiler_params=pltpu.CompilerParams(vmem_limit_bytes=58 << 20),
        cost_estimate=pl.CostEstimate(
            flops=6 * ROWS * D * units, bytes_accessed=8 << 20, transcendentals=ROWS * units
        ),
        name="feed_forward",
    )(place, x, weights)


def on_device(
    residual_in,
    query_rows,
    key_rows,
    value_rows,
    lengths,
    norm_gain,
    gate_weight,
    up_weight,
    down_weight,
):
    yh = lax.axis_index("yh")
    half = gate_weight.shape[1] // 2

    packed = jnp.concatenate([gate_weight, up_weight, down_weight.T], axis=0)
    parity = yh & 1
    mine = lax.dynamic_slice_in_dim(packed, parity * half, half, 1)
    other = lax.dynamic_slice_in_dim(packed, (1 - parity) * half, half, 1)
    near = jnp.stack(
        [mine, around(other, "yh", 1), around(mine, "yh", 2), around(other, "yh", 3)]
    )
    weights = lax.all_gather(near, ("x", "z"), axis=0)

    tail = jnp.broadcast_to(
        jnp.repeat(lengths.astype(BF16), 8)[:, None], (16, key_rows.shape[1])
    )
    k0 = jnp.concatenate([key_rows, tail], axis=0)
    k1, v1 = from_behind(k0, 1), from_behind(value_rows, 1)
    k2, v2 = from_behind(k1, 1), from_behind(v1, 1)

    attended, sent = attention(
        lengths, norm_gain[None, :], query_rows, k0, value_rows, k1, v1, k2, v2, residual_in
    )

    partner = swap(sent, "yh")
    parts = []
    for start in (sent, partner):
        chip = swap(start, "yl")
        parts += [start, swap(start, "c"), chip, swap(chip, "c")]
    own = 2 * lax.axis_index("yl") + lax.axis_index("c")
    place = [own, own ^ 1, own ^ 2, own ^ 3] + [(yh - y) & 3 for y in range(4)]
    place = jnp.stack(place).astype(jnp.int32)
    own_x, partner_x = normalize(parts)
    partner_keep, partner_send = feed_forward(place, partner_x, weights)
    own_x, partner_send = lax.optimization_barrier((own_x, partner_send))
    own_keep, own_send = feed_forward(place, own_x, weights)

    def add(left, right):
        return left.astype(F32) + right.astype(F32)

    partner_got = swap(partner_send, "c")
    own_got = swap(own_send, "c")
    partner_far = swap(add(partner_keep[0], partner_got[0]).astype(BF16), "yl")
    own_far = swap(add(own_keep[0], own_got[0]).astype(BF16), "yl")
    back = swap((add(partner_keep[1], partner_got[1]) + partner_far.astype(F32)).astype(BF16), "yh")
    summed = add(own_keep[1], own_got[1]) + own_far.astype(F32) + back.astype(F32)
    mixed = residual_in + attended.astype(F32) + summed
    return attended, mixed


def solution(mesh):
    fine = Mesh(mesh.devices.reshape(4, 8, 4, 2, 2), SEQ + TP)
    placed = (
        P(SEQ, TP),
        P(SEQ, TP),
        P(SEQ, TP),
        P(SEQ, TP),
        P(SEQ),
        P(TP),
        P(SEQ, TP),
        P(SEQ, TP),
        P(TP, SEQ),
    )
    return jax.shard_map(
        on_device,
        mesh=fine,
        in_specs=placed,
        out_specs=(P(SEQ, TP), P(SEQ, TP)),
        check_vma=False,
    )
```

```python
import math

import jax
import jax.numpy as jnp
from jax import lax
from jax.experimental import pallas as pl
from jax.experimental.pallas import tpu as pltpu
from jax.sharding import Mesh
from jax.sharding import PartitionSpec as P

D = 2048
HEAD_DIM = 128
SEG = 128
ROWS = 256
TP_WIDTH = 512
UNIT_BLOCK = 256
EXTRA = 16
epsilon = 1e-06

SEQ = ("xh", "xl", "z", "yh")
TP = ("yl", "c")
F32 = jnp.float32
BF16 = jnp.bfloat16


def from_behind(value, by):
    size = lax.axis_size(SEQ)
    return lax.ppermute(value, SEQ, [(i, i + by) for i in range(size - by)])


def around(value, axis, by):
    size = lax.axis_size(axis)
    return lax.ppermute(value, axis, [(i, (i + by) % size) for i in range(size)])


def swap(value, axis):
    size = lax.axis_size(axis)
    return lax.ppermute(value, axis, [(i, i ^ 1) for i in range(size)])


def attention_kernel(
    lengths_ref, gain_ref, *refs
):
    outside, (att_ref, send_ref), inside, sems = refs[:8], refs[8:10], refs[10:18], refs[18]
    copies = [
        pltpu.make_async_copy(src, dst, sems.at[i])
        for i, (src, dst) in enumerate(zip(outside, inside))
    ]
    for copy in copies:
        copy.start()
    q_ref, k0_ref, v0_ref, k1_ref, v1_ref, k2_ref, v2_ref, res_ref = inside
    gain = gain_ref[...]
    high = gain.astype(BF16).astype(F32)
    middle = (gain - high).astype(BF16).astype(F32)
    low = gain - high - middle
    extra = lax.broadcasted_iota(jnp.int32, (EXTRA, TP_WIDTH), 0)
    extra = jnp.where(extra == 0, high, jnp.where(extra == 1, middle, jnp.where(extra == 2, low, 0.0)))
    send_ref[pl.ds(ROWS, EXTRA), :] = extra.astype(BF16)
    for copy in copies:
        copy.wait()
    rows = lax.broadcasted_iota(jnp.int32, (ROWS, ROWS), 0)
    cols = lax.broadcasted_iota(jnp.int32, (ROWS, ROWS), 1)
    col = lax.broadcasted_iota(jnp.int32, (1, ROWS), 1)

    def valid(key_ref):
        first = key_ref[pl.ds(ROWS, 8), pl.ds(0, ROWS)].astype(F32)[0:1, :].astype(jnp.int32)
        second = key_ref[pl.ds(ROWS + 8, 8), pl.ds(0, ROWS)].astype(F32)[0:1, :].astype(jnp.int32)
        return (col < jnp.where(col < SEG, first, second + SEG)).astype(jnp.int32)

    allowed = (
        (valid(k0_ref) > 0) & (cols <= rows),
        (valid(k1_ref) + jnp.zeros_like(cols)) > 0,
        (valid(k2_ref) > 0) & (cols > rows),
    )
    row = lax.broadcasted_iota(jnp.int32, (ROWS, 1), 0)
    keep = row < jnp.where(row < SEG, lengths_ref[0], lengths_ref[1] + SEG)
    scale = 1.0 / math.sqrt(HEAD_DIM)
    keys = (k0_ref, k1_ref, k2_ref)
    values = (v0_ref, v1_ref, v2_ref)
    for head in range(TP_WIDTH // HEAD_DIM):
        at = pl.ds(head * HEAD_DIM, HEAD_DIM)
        query = q_ref[:, at]
        masked = []
        for key_ref, allow in zip(keys, allowed):
            scores = lax.dot_general(
                query,
                key_ref[pl.ds(0, ROWS), at],
                (((1,), (1,)), ((), ())),
                preferred_element_type=F32,
            )
            masked.append(jnp.where(allow, scores * scale, -1e30))
        top = jnp.max(jnp.maximum(jnp.maximum(masked[0], masked[1]), masked[2]), axis=1, keepdims=True)
        weights = [jnp.where(a, jnp.exp(m - top), 0.0) for a, m in zip(allowed, masked)]
        denominator = jnp.sum(weights[0] + weights[1] + weights[2], axis=1, keepdims=True)
        numerator = jnp.zeros((ROWS, HEAD_DIM), F32)
        for weight, value_ref in zip(weights, values):
            numerator += jnp.dot(weight.astype(BF16), value_ref[:, at], preferred_element_type=F32)
        out = jnp.where(keep, numerator / jnp.where(keep, denominator, 1.0), 0.0).astype(BF16)
        att_ref[:, at] = out
        send_ref[pl.ds(0, ROWS), at] = (res_ref[:, at] + out.astype(F32)).astype(BF16)


HBM = pl.BlockSpec(memory_space=pltpu.HBM)
SMEM = pl.BlockSpec(memory_space=pltpu.SMEM)


def attention(lengths, gain, q, k0, v0, k1, v1, k2, v2, residual_in):
    return pl.pallas_call(
        attention_kernel,
        out_shape=(
            jax.ShapeDtypeStruct((ROWS, TP_WIDTH), BF16),
            jax.ShapeDtypeStruct((ROWS + EXTRA, TP_WIDTH), BF16),
        ),
        in_specs=[SMEM, pl.BlockSpec()] + [HBM] * 8,
        out_specs=(pl.BlockSpec(), pl.BlockSpec()),
        scratch_shapes=[
            pltpu.VMEM(a.shape, a.dtype) for a in (q, k0, v0, k1, v1, k2, v2, residual_in)
        ]
        + [pltpu.SemaphoreType.DMA((8,))],
        compiler_params=pltpu.CompilerParams(vmem_limit_bytes=60 << 20),
        cost_estimate=pl.CostEstimate(
            flops=4 * ROWS * 3 * ROWS * TP_WIDTH, bytes_accessed=3 << 20, transcendentals=3 << 18
        ),
        name="attention",
    )(lengths, gain, q, k0, v0, k1, v1, k2, v2, residual_in)


def normalize_kernel(*refs):
    parts, out = refs[:8], refs[8]
    for g in range(2):
        square = jnp.zeros((ROWS, 1), F32)
        for p in range(4):
            value = parts[4 * g + p][pl.ds(0, ROWS), :].astype(F32)
            square += jnp.sum(value * value, axis=1, keepdims=True)
        inverse = lax.rsqrt(square / D + epsilon)
        for p in range(4):
            extra = parts[4 * g + p][pl.ds(ROWS, EXTRA), :].astype(F32)
            gain = extra[0:1] + extra[1:2] + extra[2:3]
            value = parts[4 * g + p][pl.ds(0, ROWS), :].astype(F32)
            out[p, pl.ds(g * ROWS, ROWS), :] = (value * inverse * gain).astype(BF16)


def normalize(parts):
    return pl.pallas_call(
        normalize_kernel,
        out_shape=jax.ShapeDtypeStruct((4, 2 * ROWS, TP_WIDTH), BF16),
        compiler_params=pltpu.CompilerParams(vmem_limit_bytes=32 << 20),
        cost_estimate=pl.CostEstimate(flops=8 * ROWS * D, bytes_accessed=4 << 20, transcendentals=0),
        name="normalize",
    )(*parts)


def feed_forward_kernel(place_ref, x_hbm, w_hbm, *refs):
    outs, (x_ref, w_ref, gate_ref, up_ref, hidden_ref, sems) = refs[:4], refs[4:]
    copies = [pltpu.make_async_copy(x_hbm, x_ref, sems.at[2])] + [
        pltpu.make_async_copy(w_hbm.at[pl.ds(place_ref[j] * 8, 8)], w_ref.at[j], sems.at[j])
        for j in range(2)
    ]
    for copy in copies:
        copy.start()

    def block(p, kind, low, width):
        pieces = [
            w_ref[
                p % 2,
                :,
                pl.ds(place_ref[6 + y], 1),
                pl.ds(place_ref[2 + p], 1),
                pl.ds(kind * 16, 16),
                pl.ds(low, width),
            ]
            for y in range(4)
        ]
        return jnp.concatenate(pieces, axis=1).reshape(TP_WIDTH, width)

    units = w_ref.shape[5]
    copies[0].wait()
    for j in range(2):
        copies[1 + j].wait()
        for low in range(0, units, UNIT_BLOCK):
            at = pl.ds(low, UNIT_BLOCK)
            for kind, total_ref in ((0, gate_ref), (1, up_ref)):
                total = jnp.dot(
                    x_ref[j], block(j, kind, low, UNIT_BLOCK), preferred_element_type=F32
                ) + jnp.dot(
                    x_ref[j + 2], block(j + 2, kind, low, UNIT_BLOCK), preferred_element_type=F32
                )
                total_ref[:, at] = total if j == 0 else total_ref[:, at] + total
    for low in range(0, units, UNIT_BLOCK):
        at = pl.ds(low, UNIT_BLOCK)
        gate = gate_ref[:, at]
        hidden_ref[:, at] = (gate / (1.0 + jnp.exp(-gate)) * up_ref[:, at]).astype(BF16)
    for i, p in enumerate((2, 0)):
        for away in (1, 0):
            product = lax.dot_general(
                hidden_ref[...],
                block(p + away, 2, 0, units),
                (((1,), (1,)), ((), ())),
                preferred_element_type=F32,
            ).astype(BF16)
            for g in range(2):
                outs[2 * g + away][i] = product[g * ROWS : (g + 1) * ROWS]


def feed_forward(place, x, weights):
    units = weights.shape[4]
    return pl.pallas_call(
        feed_forward_kernel,
        out_shape=[jax.ShapeDtypeStruct((2, ROWS, TP_WIDTH), BF16)] * 4,
        in_specs=[SMEM, HBM, HBM],
        scratch_shapes=[
            pltpu.VMEM((4, 2 * ROWS, TP_WIDTH), BF16),
            pltpu.VMEM((2, 8, 4, 2, 48, units), BF16),
            pltpu.VMEM((2 * ROWS, units), F32),
            pltpu.VMEM((2 * ROWS, units), F32),
            pltpu.VMEM((2 * ROWS, units), BF16),
            pltpu.SemaphoreType.DMA((3,)),
        ],
        compiler_params=pltpu.CompilerParams(vmem_limit_bytes=58 << 20),
        cost_estimate=pl.CostEstimate(
            flops=12 * ROWS * D * units, bytes_accessed=10 << 20, transcendentals=2 * ROWS * units
        ),
        name="feed_forward",
    )(place, x, weights)


def on_device(
    residual_in,
    query_rows,
    key_rows,
    value_rows,
    lengths,
    norm_gain,
    gate_weight,
    up_weight,
    down_weight,
):
    xh, yh = lax.axis_index("xh"), lax.axis_index("yh")
    half = gate_weight.shape[1] // 2

    packed = jnp.concatenate([gate_weight, up_weight, down_weight.T], axis=0)
    mine = lax.dynamic_slice_in_dim(packed, xh * half, half, 1)
    other = lax.dynamic_slice_in_dim(packed, (1 - xh) * half, half, 1)
    pair = jnp.stack([mine, swap(other, "xh")])
    near = jnp.stack([pair] + [around(pair, "yh", by) for by in (1, 2, 3)])
    weights = lax.all_gather(near, ("xl", "z"), axis=0)

    tail = jnp.broadcast_to(
        jnp.repeat(lengths.astype(BF16), 8)[:, None], (16, key_rows.shape[1])
    )
    k0 = jnp.concatenate([key_rows, tail], axis=0)
    k1, v1 = from_behind(k0, 1), from_behind(value_rows, 1)
    k2, v2 = from_behind(k1, 1), from_behind(v1, 1)

    attended, sent = attention(
        lengths, norm_gain[None, :], query_rows, k0, value_rows, k1, v1, k2, v2, residual_in
    )

    partner = swap(sent, "xh")
    parts = []
    for start in (sent, partner):
        chip = swap(start, "yl")
        parts += [start, swap(start, "c"), chip, swap(chip, "c")]
    own = 2 * lax.axis_index("yl") + lax.axis_index("c")
    order = [own, own ^ 1, own ^ 2, own ^ 3]
    place = [own & 1, (own & 1) ^ 1] + [(t >> 1) ^ xh for t in order] + [(yh - y) & 3 for y in range(4)]
    place = jnp.stack(place).astype(jnp.int32)
    own_keep, own_send, partner_keep, partner_send = feed_forward(place, normalize(parts), weights)

    def add(left, right):
        return left.astype(F32) + right.astype(F32)

    partner_got = swap(partner_send, "c")
    own_got = swap(own_send, "c")
    partner_far = swap(add(partner_keep[0], partner_got[0]).astype(BF16), "yl")
    own_far = swap(add(own_keep[0], own_got[0]).astype(BF16), "yl")
    back = swap((add(partner_keep[1], partner_got[1]) + partner_far.astype(F32)).astype(BF16), "xh")
    summed = add(own_keep[1], own_got[1]) + own_far.astype(F32) + back.astype(F32)
    mixed = residual_in + attended.astype(F32) + summed
    return attended, mixed


def solution(mesh):
    fine = Mesh(mesh.devices.reshape(2, 2, 8, 4, 2, 2), SEQ + TP)
    placed = (
        P(SEQ, TP),
        P(SEQ, TP),
        P(SEQ, TP),
        P(SEQ, TP),
        P(SEQ),
        P(TP),
        P(SEQ, TP),
        P(SEQ, TP),
        P(TP, SEQ),
    )
    return jax.shard_map(
        on_device,
        mesh=fine,
        in_specs=placed,
        out_specs=(P(SEQ, TP), P(SEQ, TP)),
        check_vma=False,
    )
```

```python
import math

import jax
import jax.numpy as jnp
from jax import lax
from jax.experimental import pallas as pl
from jax.experimental.pallas import tpu as pltpu
from jax.sharding import Mesh
from jax.sharding import PartitionSpec as P

D = 2048
HEAD_DIM = 128
SEG = 128
ROWS = 256
TP_WIDTH = 512
UNIT_BLOCK = 256
EXTRA = 16
epsilon = 1e-06

SEQ = ("x", "z", "yh")
TP = ("yl", "c")
F32 = jnp.float32
BF16 = jnp.bfloat16


def from_behind(value, by):
    size = lax.axis_size(SEQ)
    return lax.ppermute(value, SEQ, [(i, i + by) for i in range(size - by)])


def around(value, axis, by):
    size = lax.axis_size(axis)
    return lax.ppermute(value, axis, [(i, (i + by) % size) for i in range(size)])


def swap(value, axis):
    size = lax.axis_size(axis)
    return lax.ppermute(value, axis, [(i, i ^ 1) for i in range(size)])


def attention_kernel(
    lengths_ref, gain_ref, *refs
):
    outside, (att_ref, send_ref), inside, sems = refs[:8], refs[8:10], refs[10:18], refs[18]
    copies = [
        pltpu.make_async_copy(src, dst, sems.at[i])
        for i, (src, dst) in enumerate(zip(outside, inside))
    ]
    for copy in copies:
        copy.start()
    q_ref, k0_ref, v0_ref, k1_ref, v1_ref, k2_ref, v2_ref, res_ref = inside
    gain = gain_ref[...]
    high = gain.astype(BF16).astype(F32)
    middle = (gain - high).astype(BF16).astype(F32)
    low = gain - high - middle
    extra = lax.broadcasted_iota(jnp.int32, (EXTRA, TP_WIDTH), 0)
    extra = jnp.where(extra == 0, high, jnp.where(extra == 1, middle, jnp.where(extra == 2, low, 0.0)))
    send_ref[pl.ds(ROWS, EXTRA), :] = extra.astype(BF16)
    for copy in copies:
        copy.wait()
    rows = lax.broadcasted_iota(jnp.int32, (ROWS, ROWS), 0)
    cols = lax.broadcasted_iota(jnp.int32, (ROWS, ROWS), 1)
    col = lax.broadcasted_iota(jnp.int32, (1, ROWS), 1)

    def valid(key_ref):
        first = key_ref[pl.ds(ROWS, 8), pl.ds(0, ROWS)].astype(F32)[0:1, :].astype(jnp.int32)
        second = key_ref[pl.ds(ROWS + 8, 8), pl.ds(0, ROWS)].astype(F32)[0:1, :].astype(jnp.int32)
        return (col < jnp.where(col < SEG, first, second + SEG)).astype(jnp.int32)

    allowed = (
        (valid(k0_ref) > 0) & (cols <= rows),
        (valid(k1_ref) + jnp.zeros_like(cols)) > 0,
        (valid(k2_ref) > 0) & (cols > rows),
    )
    row = lax.broadcasted_iota(jnp.int32, (ROWS, 1), 0)
    keep = row < jnp.where(row < SEG, lengths_ref[0], lengths_ref[1] + SEG)
    scale = 1.0 / math.sqrt(HEAD_DIM)
    keys = (k0_ref, k1_ref, k2_ref)
    values = (v0_ref, v1_ref, v2_ref)
    for head in range(TP_WIDTH // HEAD_DIM):
        at = pl.ds(head * HEAD_DIM, HEAD_DIM)
        query = q_ref[:, at]
        masked = []
        for key_ref, allow in zip(keys, allowed):
            scores = lax.dot_general(
                query,
                key_ref[pl.ds(0, ROWS), at],
                (((1,), (1,)), ((), ())),
                preferred_element_type=F32,
            )
            masked.append(jnp.where(allow, scores * scale, -1e30))
        top = jnp.max(jnp.maximum(jnp.maximum(masked[0], masked[1]), masked[2]), axis=1, keepdims=True)
        weights = [jnp.where(a, jnp.exp(m - top), 0.0) for a, m in zip(allowed, masked)]
        denominator = jnp.sum(weights[0] + weights[1] + weights[2], axis=1, keepdims=True)
        numerator = jnp.zeros((ROWS, HEAD_DIM), F32)
        for weight, value_ref in zip(weights, values):
            numerator += jnp.dot(weight.astype(BF16), value_ref[:, at], preferred_element_type=F32)
        out = jnp.where(keep, numerator / jnp.where(keep, denominator, 1.0), 0.0).astype(BF16)
        att_ref[:, at] = out
        send_ref[pl.ds(0, ROWS), at] = (res_ref[:, at] + out.astype(F32)).astype(BF16)


HBM = pl.BlockSpec(memory_space=pltpu.HBM)
SMEM = pl.BlockSpec(memory_space=pltpu.SMEM)


def attention(lengths, gain, q, k0, v0, k1, v1, k2, v2, residual_in):
    return pl.pallas_call(
        attention_kernel,
        out_shape=(
            jax.ShapeDtypeStruct((ROWS, TP_WIDTH), BF16),
            jax.ShapeDtypeStruct((ROWS + EXTRA, TP_WIDTH), BF16),
        ),
        in_specs=[SMEM, pl.BlockSpec()] + [HBM] * 8,
        out_specs=(pl.BlockSpec(), pl.BlockSpec()),
        scratch_shapes=[
            pltpu.VMEM(a.shape, a.dtype) for a in (q, k0, v0, k1, v1, k2, v2, residual_in)
        ]
        + [pltpu.SemaphoreType.DMA((8,))],
        compiler_params=pltpu.CompilerParams(vmem_limit_bytes=60 << 20),
        cost_estimate=pl.CostEstimate(
            flops=4 * ROWS * 3 * ROWS * TP_WIDTH, bytes_accessed=3 << 20, transcendentals=3 << 18
        ),
        name="attention",
    )(lengths, gain, q, k0, v0, k1, v1, k2, v2, residual_in)


def normalize_kernel(*refs):
    parts, out = refs[:8], refs[8]
    for g in range(2):
        square = jnp.zeros((ROWS, 1), F32)
        for p in range(4):
            value = parts[4 * g + p][pl.ds(0, ROWS), :].astype(F32)
            square += jnp.sum(value * value, axis=1, keepdims=True)
        inverse = lax.rsqrt(square / D + epsilon)
        for p in range(4):
            extra = parts[4 * g + p][pl.ds(ROWS, EXTRA), :].astype(F32)
            gain = extra[0:1] + extra[1:2] + extra[2:3]
            value = parts[4 * g + p][pl.ds(0, ROWS), :].astype(F32)
            out[p, pl.ds(g * ROWS, ROWS), :] = (value * inverse * gain).astype(BF16)


def normalize(parts):
    return pl.pallas_call(
        normalize_kernel,
        out_shape=jax.ShapeDtypeStruct((4, 2 * ROWS, TP_WIDTH), BF16),
        compiler_params=pltpu.CompilerParams(vmem_limit_bytes=32 << 20),
        cost_estimate=pl.CostEstimate(flops=8 * ROWS * D, bytes_accessed=4 << 20, transcendentals=0),
        name="normalize",
    )(*parts)


def feed_forward_kernel(place_ref, x_hbm, *refs):
    blocks, halves, plane, outs = refs[:3], refs[3:5], refs[5], refs[6:10]
    x_ref, wide_ref, down_ref, hidden_ref, sems = refs[10:]
    pairs = [(x_hbm, x_ref)]
    pairs += [(block, wide_ref.at[place_ref[8 + i]]) for i, block in enumerate(blocks)]
    pairs += [(half, wide_ref.at[place_ref[11], pl.ds(4 * i, 4)]) for i, half in enumerate(halves)]
    pairs += [(plane.at[:, i], down_ref.at[place_ref[12 + i]]) for i in range(4)]
    copies = [pltpu.make_async_copy(src, dst, sems.at[i]) for i, (src, dst) in enumerate(pairs)]
    for copy in copies:
        copy.start()

    def load(w_ref, p, low_row, low, width):
        pieces = [
            w_ref[
                pl.ds(place_ref[p], 1),
                :,
                pl.ds(place_ref[4 + y], 1),
                pl.ds(low_row, 16),
                pl.ds(low, width),
            ]
            for y in range(4)
        ]
        return jnp.concatenate(pieces, axis=2).reshape(TP_WIDTH, width)

    units = down_ref.shape[4]
    for copy in copies[:6]:
        copy.wait()
    for low in range(0, units, UNIT_BLOCK):
        gate = jnp.zeros((2 * ROWS, UNIT_BLOCK), F32)
        up = jnp.zeros((2 * ROWS, UNIT_BLOCK), F32)
        for p in range(4):
            gate += jnp.dot(x_ref[p], load(wide_ref, p, 0, low, UNIT_BLOCK), preferred_element_type=F32)
            up += jnp.dot(x_ref[p], load(wide_ref, p, 16, low, UNIT_BLOCK), preferred_element_type=F32)
        hidden_ref[:, pl.ds(low, UNIT_BLOCK)] = (gate / (1.0 + jnp.exp(-gate)) * up).astype(BF16)
    for copy in copies[6:]:
        copy.wait()
    for i, p in enumerate((2, 0)):
        for away in (1, 0):
            product = lax.dot_general(
                hidden_ref[...],
                load(down_ref, p + away, 0, 0, units),
                (((1,), (1,)), ((), ())),
                preferred_element_type=F32,
            ).astype(BF16)
            for g in range(2):
                outs[2 * g + away][i] = product[g * ROWS : (g + 1) * ROWS]


def feed_forward(place, x, blocks, halves, plane):
    units = plane.shape[4]
    return pl.pallas_call(
        feed_forward_kernel,
        out_shape=[jax.ShapeDtypeStruct((2, ROWS, TP_WIDTH), BF16)] * 4,
        in_specs=[SMEM] + [HBM] * 7,
        scratch_shapes=[
            pltpu.VMEM((4, 2 * ROWS, TP_WIDTH), BF16),
            pltpu.VMEM((4, 8, 4, 32, units), BF16),
            pltpu.VMEM((4, 8, 4, 16, units), BF16),
            pltpu.VMEM((2 * ROWS, units), BF16),
            pltpu.SemaphoreType.DMA((10,)),
        ],
        compiler_params=pltpu.CompilerParams(vmem_limit_bytes=58 << 20),
        cost_estimate=pl.CostEstimate(
            flops=12 * ROWS * D * units, bytes_accessed=10 << 20, transcendentals=2 * ROWS * units
        ),
        name="feed_forward",
    )(place, x, *blocks, *halves, plane)


def on_device(
    residual_in,
    query_rows,
    key_rows,
    value_rows,
    lengths,
    norm_gain,
    gate_weight,
    up_weight,
    down_weight,
):
    x, yh = lax.axis_index("x"), lax.axis_index("yh")
    half = gate_weight.shape[1] // 2

    packed = jnp.concatenate([gate_weight, up_weight, down_weight.T], axis=0)
    parity = yh & 1
    mine = lax.dynamic_slice_in_dim(packed, parity * half, half, 1)
    other = lax.dynamic_slice_in_dim(packed, (1 - parity) * half, half, 1)
    near = jnp.stack(
        [mine, around(other, "yh", 1), around(mine, "yh", 2), around(other, "yh", 3)]
    )
    line = lax.all_gather(near[:, :32], "z", axis=0)
    down = near[:, 32:]
    down = jnp.stack([down] + [around(down, "x", by) for by in (1, 2, 3)])

    tail = jnp.broadcast_to(
        jnp.repeat(lengths.astype(BF16), 8)[:, None], (16, key_rows.shape[1])
    )
    k0 = jnp.concatenate([key_rows, tail], axis=0)
    k1, v1 = from_behind(k0, 1), from_behind(value_rows, 1)
    down, k1, v1 = lax.optimization_barrier((down, k1, v1))
    k2, v2 = from_behind(k1, 1), from_behind(v1, 1)
    line, k2, v2 = lax.optimization_barrier((line, k2, v2))
    plane = lax.all_gather(down, "z", axis=0)
    blocks = [line, around(line, "x", 1), around(line, "x", -1)]
    halves = [around(blocks[1][:4], "x", 1), around(blocks[2][4:], "x", -1)]

    attended, sent = attention(
        lengths, norm_gain[None, :], query_rows, k0, value_rows, k1, v1, k2, v2, residual_in
    )

    partner = swap(sent, "yh")
    parts = []
    for start in (sent, partner):
        chip = swap(start, "yl")
        parts += [start, swap(start, "c"), chip, swap(chip, "c")]
    own = 2 * lax.axis_index("yl") + lax.axis_index("c")
    place = [own, own ^ 1, own ^ 2, own ^ 3] + [(yh - y) & 3 for y in range(4)]
    place += [(x - by) & 3 for by in (0, 1, 3, 2)] + [(x - by) & 3 for by in range(4)]
    place = jnp.stack(place).astype(jnp.int32)
    own_keep, own_send, partner_keep, partner_send = feed_forward(
        place, normalize(parts), blocks, halves, plane
    )

    def add(left, right):
        return left.astype(F32) + right.astype(F32)

    partner_got = swap(partner_send, "c")
    own_got = swap(own_send, "c")
    partner_far = swap(add(partner_keep[0], partner_got[0]).astype(BF16), "yl")
    own_far = swap(add(own_keep[0], own_got[0]).astype(BF16), "yl")
    back = swap((add(partner_keep[1], partner_got[1]) + partner_far.astype(F32)).astype(BF16), "yh")
    summed = add(own_keep[1], own_got[1]) + own_far.astype(F32) + back.astype(F32)
    mixed = residual_in + attended.astype(F32) + summed
    return attended, mixed


def solution(mesh):
    fine = Mesh(mesh.devices.reshape(4, 8, 4, 2, 2), SEQ + TP)
    placed = (
        P(SEQ, TP),
        P(SEQ, TP),
        P(SEQ, TP),
        P(SEQ, TP),
        P(SEQ),
        P(TP),
        P(SEQ, TP),
        P(SEQ, TP),
        P(TP, SEQ),
    )
    return jax.shard_map(
        on_device,
        mesh=fine,
        in_specs=placed,
        out_specs=(P(SEQ, TP), P(SEQ, TP)),
        check_vma=False,
    )
```

```python
import math

import jax
import jax.numpy as jnp
from jax import lax
from jax.experimental import pallas as pl
from jax.experimental.pallas import tpu as pltpu
from jax.sharding import Mesh
from jax.sharding import PartitionSpec as P

D = 2048
HEAD_DIM = 128
SEG = 128
ROWS = 256
TP_WIDTH = 512
UNIT_BLOCK = 256
EXTRA = 16
epsilon = 1e-06

SEQ = ("x", "z", "yh")
TP = ("yl", "c")
F32 = jnp.float32
BF16 = jnp.bfloat16


def from_behind(value, by):
    size = lax.axis_size(SEQ)
    return lax.ppermute(value, SEQ, [(i, i + by) for i in range(size - by)])


def around(value, axis, by):
    size = lax.axis_size(axis)
    return lax.ppermute(value, axis, [(i, (i + by) % size) for i in range(size)])


def swap(value, axis):
    size = lax.axis_size(axis)
    return lax.ppermute(value, axis, [(i, i ^ 1) for i in range(size)])


def attention_kernel(
    lengths_ref, gain_ref, *refs
):
    outside, (att_ref, send_ref), inside, sems = refs[:8], refs[8:10], refs[10:18], refs[18]
    copies = [
        pltpu.make_async_copy(src, dst, sems.at[i])
        for i, (src, dst) in enumerate(zip(outside, inside))
    ]
    for copy in copies:
        copy.start()
    q_ref, k0_ref, v0_ref, k1_ref, v1_ref, k2_ref, v2_ref, res_ref = inside
    gain = gain_ref[...]
    high = gain.astype(BF16).astype(F32)
    middle = (gain - high).astype(BF16).astype(F32)
    low = gain - high - middle
    extra = lax.broadcasted_iota(jnp.int32, (EXTRA, TP_WIDTH), 0)
    extra = jnp.where(extra == 0, high, jnp.where(extra == 1, middle, jnp.where(extra == 2, low, 0.0)))
    send_ref[pl.ds(ROWS, EXTRA), :] = extra.astype(BF16)
    for copy in copies:
        copy.wait()
    rows = lax.broadcasted_iota(jnp.int32, (ROWS, ROWS), 0)
    cols = lax.broadcasted_iota(jnp.int32, (ROWS, ROWS), 1)
    col = lax.broadcasted_iota(jnp.int32, (1, ROWS), 1)

    def valid(key_ref):
        first = key_ref[pl.ds(ROWS, 8), pl.ds(0, ROWS)].astype(F32)[0:1, :].astype(jnp.int32)
        second = key_ref[pl.ds(ROWS + 8, 8), pl.ds(0, ROWS)].astype(F32)[0:1, :].astype(jnp.int32)
        return (col < jnp.where(col < SEG, first, second + SEG)).astype(jnp.int32)

    allowed = (
        (valid(k0_ref) > 0) & (cols <= rows),
        (valid(k1_ref) + jnp.zeros_like(cols)) > 0,
        (valid(k2_ref) > 0) & (cols > rows),
    )
    row = lax.broadcasted_iota(jnp.int32, (ROWS, 1), 0)
    keep = row < jnp.where(row < SEG, lengths_ref[0], lengths_ref[1] + SEG)
    scale = 1.0 / math.sqrt(HEAD_DIM)
    keys = (k0_ref, k1_ref, k2_ref)
    values = (v0_ref, v1_ref, v2_ref)
    for head in range(TP_WIDTH // HEAD_DIM):
        at = pl.ds(head * HEAD_DIM, HEAD_DIM)
        query = q_ref[:, at]
        masked = []
        for key_ref, allow in zip(keys, allowed):
            scores = lax.dot_general(
                query,
                key_ref[pl.ds(0, ROWS), at],
                (((1,), (1,)), ((), ())),
                preferred_element_type=F32,
            )
            masked.append(jnp.where(allow, scores * scale, -1e30))
        top = jnp.max(jnp.maximum(jnp.maximum(masked[0], masked[1]), masked[2]), axis=1, keepdims=True)
        weights = [jnp.where(a, jnp.exp(m - top), 0.0) for a, m in zip(allowed, masked)]
        denominator = jnp.sum(weights[0] + weights[1] + weights[2], axis=1, keepdims=True)
        numerator = jnp.zeros((ROWS, HEAD_DIM), F32)
        for weight, value_ref in zip(weights, values):
            numerator += jnp.dot(weight.astype(BF16), value_ref[:, at], preferred_element_type=F32)
        out = jnp.where(keep, numerator / jnp.where(keep, denominator, 1.0), 0.0).astype(BF16)
        att_ref[:, at] = out
        send_ref[pl.ds(0, ROWS), at] = (res_ref[:, at] + out.astype(F32)).astype(BF16)


HBM = pl.BlockSpec(memory_space=pltpu.HBM)
SMEM = pl.BlockSpec(memory_space=pltpu.SMEM)


def attention(lengths, gain, q, k0, v0, k1, v1, k2, v2, residual_in):
    return pl.pallas_call(
        attention_kernel,
        out_shape=(
            jax.ShapeDtypeStruct((ROWS, TP_WIDTH), BF16),
            jax.ShapeDtypeStruct((ROWS + EXTRA, TP_WIDTH), BF16),
        ),
        in_specs=[SMEM, pl.BlockSpec()] + [HBM] * 8,
        out_specs=(pl.BlockSpec(), pl.BlockSpec()),
        scratch_shapes=[
            pltpu.VMEM(a.shape, a.dtype) for a in (q, k0, v0, k1, v1, k2, v2, residual_in)
        ]
        + [pltpu.SemaphoreType.DMA((8,))],
        compiler_params=pltpu.CompilerParams(vmem_limit_bytes=60 << 20),
        cost_estimate=pl.CostEstimate(
            flops=4 * ROWS * 3 * ROWS * TP_WIDTH, bytes_accessed=3 << 20, transcendentals=3 << 18
        ),
        name="attention",
    )(lengths, gain, q, k0, v0, k1, v1, k2, v2, residual_in)


def normalize_kernel(*refs):
    parts, out = refs[:8], refs[8]
    for g in range(2):
        square = jnp.zeros((ROWS, 1), F32)
        for p in range(4):
            value = parts[4 * g + p][pl.ds(0, ROWS), :].astype(F32)
            square += jnp.sum(value * value, axis=1, keepdims=True)
        inverse = lax.rsqrt(square / D + epsilon)
        for p in range(4):
            extra = parts[4 * g + p][pl.ds(ROWS, EXTRA), :].astype(F32)
            gain = extra[0:1] + extra[1:2] + extra[2:3]
            value = parts[4 * g + p][pl.ds(0, ROWS), :].astype(F32)
            at = pl.ds(p % 2 * TP_WIDTH, TP_WIDTH)
            out[p // 2, pl.ds(g * ROWS, ROWS), at] = (value * inverse * gain).astype(BF16)


def normalize(parts):
    return pl.pallas_call(
        normalize_kernel,
        out_shape=jax.ShapeDtypeStruct((2, 2 * ROWS, 2 * TP_WIDTH), BF16),
        compiler_params=pltpu.CompilerParams(vmem_limit_bytes=32 << 20),
        cost_estimate=pl.CostEstimate(flops=8 * ROWS * D, bytes_accessed=4 << 20, transcendentals=0),
        name="normalize",
    )(*parts)


def pieces_of(w_ref, p, place_ref, low_row, low, width):
    pieces = [
        w_ref[p, :, pl.ds(place_ref[4 + y], 1), pl.ds(low_row, 16), pl.ds(low, width)]
        for y in range(4)
    ]
    return jnp.concatenate(pieces, axis=1).reshape(TP_WIDTH, width)


def down_projection(hidden_ref, rows, out_own, out_partner, i):
    product = lax.dot_general(
        hidden_ref[...], rows, (((1,), (1,)), ((), ())), preferred_element_type=F32
    ).astype(BF16)
    out_own[i] = product[:ROWS]
    out_partner[i] = product[ROWS:]


def hidden_kernel(place_ref, x_hbm, w_hbm, hidden_ref, own_ref, partner_ref, x_ref, w_ref, gate_ref, up_ref, sems):
    copies = []
    for j in range(2):
        copies.append(pltpu.make_async_copy(x_hbm.at[j], x_ref.at[j], sems.at[3 * j]))
        for p in (2 * j, 2 * j + 1):
            source = w_hbm.at[pl.ds(place_ref[p] * 8, 8)]
            copies.append(pltpu.make_async_copy(source, w_ref.at[p], sems.at[3 * j + 1 + p % 2]))
    for copy in copies:
        copy.start()
    units = w_ref.shape[4]
    for j in range(2):
        for copy in copies[3 * j : 3 * j + 3]:
            copy.wait()
        for low in range(0, units, UNIT_BLOCK):
            at = pl.ds(low, UNIT_BLOCK)
            totals = []
            for kind, total_ref in ((0, gate_ref), (1, up_ref)):
                rows = jnp.concatenate(
                    [pieces_of(w_ref, 2 * j + i, place_ref, 16 * kind, low, UNIT_BLOCK) for i in range(2)],
                    axis=0,
                )
                total = jnp.dot(x_ref[j], rows, preferred_element_type=F32)
                if j == 0:
                    total_ref[:, at] = total
                else:
                    totals.append(total_ref[:, at] + total)
            if j == 1:
                gate, up = totals
                hidden_ref[:, at] = (gate / (1.0 + jnp.exp(-gate)) * up).astype(BF16)
    for i, p in enumerate((3, 1)):
        rows = pieces_of(w_ref, p, place_ref, 32, 0, units)
        down_projection(hidden_ref, rows, own_ref, partner_ref, i)


def keep_kernel(place_ref, hidden_hbm, w_hbm, own_ref, partner_ref, hidden_ref, w_ref, sems):
    copies = [pltpu.make_async_copy(hidden_hbm, hidden_ref, sems.at[2])]
    for i, p in enumerate((2, 0)):
        source = w_hbm.at[pl.ds(place_ref[p] * 8, 8), :, pl.ds(32, 16)]
        copies.append(pltpu.make_async_copy(source, w_ref.at[i], sems.at[i]))
    for copy in copies:
        copy.start()
    for copy in copies:
        copy.wait()
    for i in range(2):
        rows = pieces_of(w_ref, i, place_ref, 0, 0, w_ref.shape[4])
        down_projection(hidden_ref, rows, own_ref, partner_ref, i)


def feed_forward(place, x, weights):
    units = weights.shape[3]
    pair = jax.ShapeDtypeStruct((2, ROWS, TP_WIDTH), BF16)
    flops = 4 * ROWS * D * units
    hidden, own_send, partner_send = pl.pallas_call(
        hidden_kernel,
        out_shape=(jax.ShapeDtypeStruct((2 * ROWS, units), BF16), pair, pair),
        in_specs=[SMEM, HBM, HBM],
        scratch_shapes=[
            pltpu.VMEM((2, 2 * ROWS, 2 * TP_WIDTH), BF16),
            pltpu.VMEM((4, 8, 4, 48, units), BF16),
            pltpu.VMEM((2 * ROWS, units), F32),
            pltpu.VMEM((2 * ROWS, units), F32),
            pltpu.SemaphoreType.DMA((6,)),
        ],
        compiler_params=pltpu.CompilerParams(vmem_limit_bytes=58 << 20),
        cost_estimate=pl.CostEstimate(
            flops=5 * flops // 2, bytes_accessed=10 << 20, transcendentals=2 * ROWS * units
        ),
        name="hidden",
    )(place, x, weights)
    own_keep, partner_keep = pl.pallas_call(
        keep_kernel,
        out_shape=(pair, pair),
        in_specs=[SMEM, HBM, HBM],
        scratch_shapes=[
            pltpu.VMEM((2 * ROWS, units), BF16),
            pltpu.VMEM((2, 8, 4, 16, units), BF16),
            pltpu.SemaphoreType.DMA((3,)),
        ],
        compiler_params=pltpu.CompilerParams(vmem_limit_bytes=58 << 20),
        cost_estimate=pl.CostEstimate(flops=flops // 2, bytes_accessed=3 << 20, transcendentals=0),
        name="keep",
    )(place, hidden, weights)
    return own_keep, own_send, partner_keep, partner_send


def on_device(
    residual_in,
    query_rows,
    key_rows,
    value_rows,
    lengths,
    norm_gain,
    gate_weight,
    up_weight,
    down_weight,
):
    yh = lax.axis_index("yh")
    half = gate_weight.shape[1] // 2

    packed = jnp.concatenate([gate_weight, up_weight, down_weight.T], axis=0)
    parity = yh & 1
    mine = lax.dynamic_slice_in_dim(packed, parity * half, half, 1)
    other = lax.dynamic_slice_in_dim(packed, (1 - parity) * half, half, 1)
    near = jnp.stack(
        [mine, around(other, "yh", 1), around(mine, "yh", 2), around(other, "yh", 3)]
    )
    weights = lax.all_gather(near, ("x", "z"), axis=0)

    tail = jnp.broadcast_to(
        jnp.repeat(lengths.astype(BF16), 8)[:, None], (16, key_rows.shape[1])
    )
    k0 = jnp.concatenate([key_rows, tail], axis=0)
    k1, v1 = from_behind(k0, 1), from_behind(value_rows, 1)
    k2, v2 = from_behind(k1, 1), from_behind(v1, 1)

    attended, sent = attention(
        lengths, norm_gain[None, :], query_rows, k0, value_rows, k1, v1, k2, v2, residual_in
    )

    partner = swap(sent, "yh")
    parts = []
    for start in (sent, partner):
        chip = swap(start, "yl")
        parts += [start, swap(start, "c"), chip, swap(chip, "c")]
    own = 2 * lax.axis_index("yl") + lax.axis_index("c")
    place = [own, own ^ 1, own ^ 2, own ^ 3] + [(yh - y) & 3 for y in range(4)]
    place = jnp.stack(place).astype(jnp.int32)
    own_keep, own_send, partner_keep, partner_send = feed_forward(
        place, normalize(parts), weights
    )

    def add(left, right):
        return left.astype(F32) + right.astype(F32)

    partner_got = swap(partner_send, "c")
    own_got = swap(own_send, "c")
    partner_far = swap(add(partner_keep[0], partner_got[0]).astype(BF16), "yl")
    own_far = swap(add(own_keep[0], own_got[0]).astype(BF16), "yl")
    back = swap((add(partner_keep[1], partner_got[1]) + partner_far.astype(F32)).astype(BF16), "yh")
    summed = add(own_keep[1], own_got[1]) + own_far.astype(F32) + back.astype(F32)
    mixed = residual_in + attended.astype(F32) + summed
    return attended, mixed


def solution(mesh):
    fine = Mesh(mesh.devices.reshape(4, 8, 4, 2, 2), SEQ + TP)
    placed = (
        P(SEQ, TP),
        P(SEQ, TP),
        P(SEQ, TP),
        P(SEQ, TP),
        P(SEQ),
        P(TP),
        P(SEQ, TP),
        P(SEQ, TP),
        P(TP, SEQ),
    )
    return jax.shard_map(
        on_device,
        mesh=fine,
        in_specs=placed,
        out_specs=(P(SEQ, TP), P(SEQ, TP)),
        check_vma=False,
    )
```

```python
import math

import jax
import jax.numpy as jnp
from jax import lax
from jax.experimental import pallas as pl
from jax.experimental.pallas import tpu as pltpu
from jax.sharding import Mesh
from jax.sharding import PartitionSpec as P

D = 2048
HEAD_DIM = 128
SEG = 128
ROWS = 256
TP_WIDTH = 512
UNIT_BLOCK = 256
EXTRA = 16
epsilon = 1e-06

SEQ = ("x", "z", "yh")
TP = ("yl", "c")
F32 = jnp.float32
BF16 = jnp.bfloat16


def from_behind(value, by):
    size = lax.axis_size(SEQ)
    return lax.ppermute(value, SEQ, [(i, i + by) for i in range(size - by)])


def around(value, axis, by):
    size = lax.axis_size(axis)
    return lax.ppermute(value, axis, [(i, (i + by) % size) for i in range(size)])


def swap(value, axis):
    size = lax.axis_size(axis)
    return lax.ppermute(value, axis, [(i, i ^ 1) for i in range(size)])


def attention_kernel(
    lengths_ref, gain_ref, *refs
):
    outside, (att_ref, send_ref), inside, sems = refs[:8], refs[8:10], refs[10:18], refs[18]
    copies = [
        pltpu.make_async_copy(src, dst, sems.at[i])
        for i, (src, dst) in enumerate(zip(outside, inside))
    ]
    for copy in copies:
        copy.start()
    q_ref, k0_ref, v0_ref, k1_ref, v1_ref, k2_ref, v2_ref, res_ref = inside
    gain = gain_ref[...]
    high = gain.astype(BF16).astype(F32)
    middle = (gain - high).astype(BF16).astype(F32)
    low = gain - high - middle
    extra = lax.broadcasted_iota(jnp.int32, (EXTRA, TP_WIDTH), 0)
    extra = jnp.where(extra == 0, high, jnp.where(extra == 1, middle, jnp.where(extra == 2, low, 0.0)))
    send_ref[pl.ds(ROWS, EXTRA), :] = extra.astype(BF16)
    for copy in copies:
        copy.wait()
    rows = lax.broadcasted_iota(jnp.int32, (ROWS, ROWS), 0)
    cols = lax.broadcasted_iota(jnp.int32, (ROWS, ROWS), 1)
    col = lax.broadcasted_iota(jnp.int32, (1, ROWS), 1)

    def valid(key_ref):
        first = key_ref[pl.ds(ROWS, 8), pl.ds(0, ROWS)].astype(F32)[0:1, :].astype(jnp.int32)
        second = key_ref[pl.ds(ROWS + 8, 8), pl.ds(0, ROWS)].astype(F32)[0:1, :].astype(jnp.int32)
        return (col < jnp.where(col < SEG, first, second + SEG)).astype(jnp.int32)

    allowed = (
        (valid(k0_ref) > 0) & (cols <= rows),
        (valid(k1_ref) + jnp.zeros_like(cols)) > 0,
        (valid(k2_ref) > 0) & (cols > rows),
    )
    row = lax.broadcasted_iota(jnp.int32, (ROWS, 1), 0)
    keep = row < jnp.where(row < SEG, lengths_ref[0], lengths_ref[1] + SEG)
    scale = 1.0 / math.sqrt(HEAD_DIM)
    keys = (k0_ref, k1_ref, k2_ref)
    values = (v0_ref, v1_ref, v2_ref)
    for head in range(TP_WIDTH // HEAD_DIM):
        at = pl.ds(head * HEAD_DIM, HEAD_DIM)
        query = q_ref[:, at]
        masked = []
        for key_ref, allow in zip(keys, allowed):
            scores = lax.dot_general(
                query,
                key_ref[pl.ds(0, ROWS), at],
                (((1,), (1,)), ((), ())),
                preferred_element_type=F32,
            )
            masked.append(jnp.where(allow, scores * scale, -1e30))
        top = jnp.max(jnp.maximum(jnp.maximum(masked[0], masked[1]), masked[2]), axis=1, keepdims=True)
        weights = [jnp.where(a, jnp.exp(m - top), 0.0) for a, m in zip(allowed, masked)]
        denominator = jnp.sum(weights[0] + weights[1] + weights[2], axis=1, keepdims=True)
        numerator = jnp.zeros((ROWS, HEAD_DIM), F32)
        for weight, value_ref in zip(weights, values):
            numerator += jnp.dot(weight.astype(BF16), value_ref[:, at], preferred_element_type=F32)
        out = jnp.where(keep, numerator / jnp.where(keep, denominator, 1.0), 0.0).astype(BF16)
        att_ref[:, at] = out
        send_ref[pl.ds(0, ROWS), at] = (res_ref[:, at] + out.astype(F32)).astype(BF16)


HBM = pl.BlockSpec(memory_space=pltpu.HBM)
SMEM = pl.BlockSpec(memory_space=pltpu.SMEM)


def attention(lengths, gain, q, k0, v0, k1, v1, k2, v2, residual_in):
    return pl.pallas_call(
        attention_kernel,
        out_shape=(
            jax.ShapeDtypeStruct((ROWS, TP_WIDTH), BF16),
            jax.ShapeDtypeStruct((ROWS + EXTRA, TP_WIDTH), BF16),
        ),
        in_specs=[SMEM, pl.BlockSpec()] + [HBM] * 8,
        out_specs=(pl.BlockSpec(), pl.BlockSpec()),
        scratch_shapes=[
            pltpu.VMEM(a.shape, a.dtype) for a in (q, k0, v0, k1, v1, k2, v2, residual_in)
        ]
        + [pltpu.SemaphoreType.DMA((8,))],
        compiler_params=pltpu.CompilerParams(vmem_limit_bytes=60 << 20),
        cost_estimate=pl.CostEstimate(
            flops=4 * ROWS * 3 * ROWS * TP_WIDTH, bytes_accessed=3 << 20, transcendentals=3 << 18
        ),
        name="attention",
    )(lengths, gain, q, k0, v0, k1, v1, k2, v2, residual_in)


def normalize_kernel(*refs):
    parts, out = refs[:8], refs[8]
    for g in range(2):
        square = jnp.zeros((ROWS, 1), F32)
        for p in range(4):
            value = parts[4 * g + p][pl.ds(0, ROWS), :].astype(F32)
            square += jnp.sum(value * value, axis=1, keepdims=True)
        inverse = lax.rsqrt(square / D + epsilon)
        for p in range(4):
            extra = parts[4 * g + p][pl.ds(ROWS, EXTRA), :].astype(F32)
            gain = extra[0:1] + extra[1:2] + extra[2:3]
            value = parts[4 * g + p][pl.ds(0, ROWS), :].astype(F32)
            out[p, pl.ds(g * ROWS, ROWS), :] = (value * inverse * gain).astype(BF16)


def normalize(parts):
    return pl.pallas_call(
        normalize_kernel,
        out_shape=jax.ShapeDtypeStruct((4, 2 * ROWS, TP_WIDTH), BF16),
        compiler_params=pltpu.CompilerParams(vmem_limit_bytes=32 << 20),
        cost_estimate=pl.CostEstimate(flops=8 * ROWS * D, bytes_accessed=4 << 20, transcendentals=0),
        name="normalize",
    )(*parts)


def feed_forward_kernel(place_ref, x_ref, w_ref, *refs):
    outs, acc_ref = refs[:4], refs[4]
    step = pl.program_id(0)

    def block(p, kind):
        pieces = [
            w_ref[
                pl.ds(place_ref[p] * 8, 8),
                pl.ds(place_ref[4 + y], 1),
                pl.ds(kind * 16, 16),
                :,
            ]
            for y in range(4)
        ]
        return jnp.concatenate(pieces, axis=1).reshape(TP_WIDTH, UNIT_BLOCK)

    gate = jnp.zeros((2 * ROWS, UNIT_BLOCK), F32)
    up = jnp.zeros((2 * ROWS, UNIT_BLOCK), F32)
    for p in range(4):
        gate += jnp.dot(x_ref[p], block(p, 0), preferred_element_type=F32)
        up += jnp.dot(x_ref[p], block(p, 1), preferred_element_type=F32)
    hidden = (gate / (1.0 + jnp.exp(-gate)) * up).astype(BF16)

    def down(p):
        return lax.dot_general(
            hidden, block(p, 2), (((1,), (1,)), ((), ())), preferred_element_type=F32
        )

    @pl.when(step == 0)
    def _():
        for p in range(4):
            acc_ref[p] = down(p)

    @pl.when(step == 1)
    def _():
        for i, p in enumerate((2, 0)):
            for away in range(2):
                total = (acc_ref[p + away] + down(p + away)).astype(BF16)
                for g in range(2):
                    outs[2 * g + away][i] = total[g * ROWS : (g + 1) * ROWS]


def feed_forward(place, x, weights):
    pair = pl.BlockSpec((2, ROWS, TP_WIDTH), lambda i, o: (0, 0, 0))
    units = weights.shape[3]
    assert units == 2 * UNIT_BLOCK
    return pl.pallas_call(
        feed_forward_kernel,
        out_shape=[jax.ShapeDtypeStruct((2, ROWS, TP_WIDTH), BF16)] * 4,
        grid_spec=pltpu.PrefetchScalarGridSpec(
            num_scalar_prefetch=1,
            grid=(2,),
            in_specs=[
                pl.BlockSpec((4, 2 * ROWS, TP_WIDTH), lambda i, o: (0, 0, 0)),
                pl.BlockSpec((32, 4, 48, UNIT_BLOCK), lambda i, o: (0, 0, 0, i)),
            ],
            out_specs=[pair] * 4,
            scratch_shapes=[pltpu.VMEM((4, 2 * ROWS, TP_WIDTH), F32)],
        ),
        compiler_params=pltpu.CompilerParams(vmem_limit_bytes=48 << 20),
        cost_estimate=pl.CostEstimate(
            flops=12 * ROWS * D * units, bytes_accessed=10 << 20, transcendentals=2 * ROWS * units
        ),
        name="feed_forward",
    )(place, x, weights)


def on_device(
    residual_in,
    query_rows,
    key_rows,
    value_rows,
    lengths,
    norm_gain,
    gate_weight,
    up_weight,
    down_weight,
):
    yh = lax.axis_index("yh")
    half = gate_weight.shape[1] // 2

    packed = jnp.concatenate([gate_weight, up_weight, down_weight.T], axis=0)
    parity = yh & 1
    mine = lax.dynamic_slice_in_dim(packed, parity * half, half, 1)
    other = lax.dynamic_slice_in_dim(packed, (1 - parity) * half, half, 1)
    near = jnp.stack(
        [mine, around(other, "yh", 1), around(mine, "yh", 2), around(other, "yh", 3)]
    )
    weights = lax.all_gather(near, ("x", "z"), axis=0)

    tail = jnp.broadcast_to(
        jnp.repeat(lengths.astype(BF16), 8)[:, None], (16, key_rows.shape[1])
    )
    k0 = jnp.concatenate([key_rows, tail], axis=0)
    k1, v1 = from_behind(k0, 1), from_behind(value_rows, 1)
    k2, v2 = from_behind(k1, 1), from_behind(v1, 1)

    attended, sent = attention(
        lengths, norm_gain[None, :], query_rows, k0, value_rows, k1, v1, k2, v2, residual_in
    )

    partner = swap(sent, "yh")
    parts = []
    for start in (sent, partner):
        chip = swap(start, "yl")
        parts += [start, swap(start, "c"), chip, swap(chip, "c")]
    own = 2 * lax.axis_index("yl") + lax.axis_index("c")
    place = [own, own ^ 1, own ^ 2, own ^ 3] + [(yh - y) & 3 for y in range(4)]
    place = jnp.stack(place).astype(jnp.int32)
    own_keep, own_send, partner_keep, partner_send = feed_forward(
        place, normalize(parts), weights
    )

    def add(left, right):
        return left.astype(F32) + right.astype(F32)

    partner_got = swap(partner_send, "c")
    own_got = swap(own_send, "c")
    partner_far = swap(add(partner_keep[0], partner_got[0]).astype(BF16), "yl")
    own_far = swap(add(own_keep[0], own_got[0]).astype(BF16), "yl")
    back = swap((add(partner_keep[1], partner_got[1]) + partner_far.astype(F32)).astype(BF16), "yh")
    summed = add(own_keep[1], own_got[1]) + own_far.astype(F32) + back.astype(F32)
    mixed = residual_in + attended.astype(F32) + summed
    return attended, mixed


def solution(mesh):
    fine = Mesh(mesh.devices.reshape(4, 8, 4, 2, 2), SEQ + TP)
    placed = (
        P(SEQ, TP),
        P(SEQ, TP),
        P(SEQ, TP),
        P(SEQ, TP),
        P(SEQ),
        P(TP),
        P(SEQ, TP),
        P(SEQ, TP),
        P(TP, SEQ),
    )
    return jax.shard_map(
        on_device,
        mesh=fine,
        in_specs=placed,
        out_specs=(P(SEQ, TP), P(SEQ, TP)),
        check_vma=False,
    )
```

```python
import math

import jax
import jax.numpy as jnp
from jax import lax
from jax.experimental import pallas as pl
from jax.experimental.pallas import tpu as pltpu
from jax.sharding import Mesh
from jax.sharding import PartitionSpec as P

D = 2048
HEAD_DIM = 128
SEG = 128
ROWS = 256
TP_WIDTH = 512
UNIT_BLOCK = 256
EXTRA = 16
epsilon = 1e-06

SEQ = ("x", "z", "yh")
TP = ("yl", "c")
F32 = jnp.float32
BF16 = jnp.bfloat16


def from_behind(value, by):
    size = lax.axis_size(SEQ)
    return lax.ppermute(value, SEQ, [(i, i + by) for i in range(size - by)])


def swap(value, axis):
    size = lax.axis_size(axis)
    return lax.ppermute(value, axis, [(i, i ^ 1) for i in range(size)])


def attention_kernel(
    lengths_ref, gain_ref, *refs
):
    outside, (att_ref, send_ref), inside, sems = refs[:8], refs[8:10], refs[10:18], refs[18]
    copies = [
        pltpu.make_async_copy(src, dst, sems.at[i])
        for i, (src, dst) in enumerate(zip(outside, inside))
    ]
    for copy in copies:
        copy.start()
    q_ref, k0_ref, v0_ref, k1_ref, v1_ref, k2_ref, v2_ref, res_ref = inside
    gain = gain_ref[...]
    high = gain.astype(BF16).astype(F32)
    middle = (gain - high).astype(BF16).astype(F32)
    low = gain - high - middle
    extra = lax.broadcasted_iota(jnp.int32, (EXTRA, TP_WIDTH), 0)
    extra = jnp.where(extra == 0, high, jnp.where(extra == 1, middle, jnp.where(extra == 2, low, 0.0)))
    send_ref[pl.ds(ROWS, EXTRA), :] = extra.astype(BF16)
    for copy in copies:
        copy.wait()
    rows = lax.broadcasted_iota(jnp.int32, (ROWS, ROWS), 0)
    cols = lax.broadcasted_iota(jnp.int32, (ROWS, ROWS), 1)
    col = lax.broadcasted_iota(jnp.int32, (1, ROWS), 1)

    def valid(key_ref):
        first = key_ref[pl.ds(ROWS, 8), pl.ds(0, ROWS)].astype(F32)[0:1, :].astype(jnp.int32)
        second = key_ref[pl.ds(ROWS + 8, 8), pl.ds(0, ROWS)].astype(F32)[0:1, :].astype(jnp.int32)
        return (col < jnp.where(col < SEG, first, second + SEG)).astype(jnp.int32)

    allowed = (
        (valid(k0_ref) > 0) & (cols <= rows),
        (valid(k1_ref) + jnp.zeros_like(cols)) > 0,
        (valid(k2_ref) > 0) & (cols > rows),
    )
    row = lax.broadcasted_iota(jnp.int32, (ROWS, 1), 0)
    keep = row < jnp.where(row < SEG, lengths_ref[0], lengths_ref[1] + SEG)
    scale = 1.0 / math.sqrt(HEAD_DIM)
    keys = (k0_ref, k1_ref, k2_ref)
    values = (v0_ref, v1_ref, v2_ref)
    for head in range(TP_WIDTH // HEAD_DIM):
        at = pl.ds(head * HEAD_DIM, HEAD_DIM)
        query = q_ref[:, at]
        masked = []
        for key_ref, allow in zip(keys, allowed):
            scores = lax.dot_general(
                query,
                key_ref[pl.ds(0, ROWS), at],
                (((1,), (1,)), ((), ())),
                preferred_element_type=F32,
            )
            masked.append(jnp.where(allow, scores * scale, -1e30))
        top = jnp.max(jnp.maximum(jnp.maximum(masked[0], masked[1]), masked[2]), axis=1, keepdims=True)
        weights = [jnp.where(a, jnp.exp(m - top), 0.0) for a, m in zip(allowed, masked)]
        denominator = jnp.sum(weights[0] + weights[1] + weights[2], axis=1, keepdims=True)
        numerator = jnp.zeros((ROWS, HEAD_DIM), F32)
        for weight, value_ref in zip(weights, values):
            numerator += jnp.dot(weight.astype(BF16), value_ref[:, at], preferred_element_type=F32)
        out = jnp.where(keep, numerator / jnp.where(keep, denominator, 1.0), 0.0).astype(BF16)
        att_ref[:, at] = out
        send_ref[pl.ds(0, ROWS), at] = (res_ref[:, at] + out.astype(F32)).astype(BF16)


HBM = pl.BlockSpec(memory_space=pltpu.HBM)
SMEM = pl.BlockSpec(memory_space=pltpu.SMEM)


def attention(lengths, gain, q, k0, v0, k1, v1, k2, v2, residual_in):
    return pl.pallas_call(
        attention_kernel,
        out_shape=(
            jax.ShapeDtypeStruct((ROWS, TP_WIDTH), BF16),
            jax.ShapeDtypeStruct((ROWS + EXTRA, TP_WIDTH), BF16),
        ),
        in_specs=[SMEM, pl.BlockSpec()] + [HBM] * 8,
        out_specs=(pl.BlockSpec(), pl.BlockSpec()),
        scratch_shapes=[
            pltpu.VMEM(a.shape, a.dtype) for a in (q, k0, v0, k1, v1, k2, v2, residual_in)
        ]
        + [pltpu.SemaphoreType.DMA((8,))],
        compiler_params=pltpu.CompilerParams(vmem_limit_bytes=60 << 20),
        cost_estimate=pl.CostEstimate(
            flops=4 * ROWS * 3 * ROWS * TP_WIDTH, bytes_accessed=3 << 20, transcendentals=3 << 18
        ),
        name="attention",
    )(lengths, gain, q, k0, v0, k1, v1, k2, v2, residual_in)


def normalize_kernel(*refs):
    parts, out = refs[:8], refs[8]
    for g in range(2):
        square = jnp.zeros((ROWS, 1), F32)
        for p in range(4):
            value = parts[4 * g + p][pl.ds(0, ROWS), :].astype(F32)
            square += jnp.sum(value * value, axis=1, keepdims=True)
        inverse = lax.rsqrt(square / D + epsilon)
        for p in range(4):
            extra = parts[4 * g + p][pl.ds(ROWS, EXTRA), :].astype(F32)
            gain = extra[0:1] + extra[1:2] + extra[2:3]
            value = parts[4 * g + p][pl.ds(0, ROWS), :].astype(F32)
            out[p, pl.ds(g * ROWS, ROWS), :] = (value * inverse * gain).astype(BF16)


def normalize(parts):
    return pl.pallas_call(
        normalize_kernel,
        out_shape=jax.ShapeDtypeStruct((4, 2 * ROWS, TP_WIDTH), BF16),
        compiler_params=pltpu.CompilerParams(vmem_limit_bytes=32 << 20),
        cost_estimate=pl.CostEstimate(flops=8 * ROWS * D, bytes_accessed=4 << 20, transcendentals=0),
        name="normalize",
    )(*parts)


def feed_forward_kernel(place_ref, x_ref, w_ref, *refs):
    outs, acc_ref = refs[:4], refs[4]
    step = pl.program_id(0)

    def block(p, kind):
        pieces = [
            w_ref[
                pl.ds(place_ref[p] * 8, 8),
                pl.ds(y, 1),
                pl.ds(kind * 16, 16),
                :,
            ]
            for y in range(4)
        ]
        return jnp.concatenate(pieces, axis=1).reshape(TP_WIDTH, UNIT_BLOCK)

    gate = jnp.zeros((2 * ROWS, UNIT_BLOCK), F32)
    up = jnp.zeros((2 * ROWS, UNIT_BLOCK), F32)
    for p in range(4):
        gate += jnp.dot(x_ref[p], block(p, 0), preferred_element_type=F32)
        up += jnp.dot(x_ref[p], block(p, 1), preferred_element_type=F32)
    hidden = (gate / (1.0 + jnp.exp(-gate)) * up).astype(BF16)

    def down(p):
        return lax.dot_general(
            hidden, block(p, 2), (((1,), (1,)), ((), ())), preferred_element_type=F32
        )

    @pl.when(step == 0)
    def _():
        for p in range(4):
            acc_ref[p] = down(p)

    @pl.when(step == 1)
    def _():
        for i, p in enumerate((2, 0)):
            for away in range(2):
                total = (acc_ref[p + away] + down(p + away)).astype(BF16)
                for g in range(2):
                    outs[2 * g + away][i] = total[g * ROWS : (g + 1) * ROWS]


def feed_forward(place, x, weights):
    pair = pl.BlockSpec((2, ROWS, TP_WIDTH), lambda i, o: (0, 0, 0))
    units = weights.shape[3]
    assert units == 2 * UNIT_BLOCK
    return pl.pallas_call(
        feed_forward_kernel,
        out_shape=[jax.ShapeDtypeStruct((2, ROWS, TP_WIDTH), BF16)] * 4,
        grid_spec=pltpu.PrefetchScalarGridSpec(
            num_scalar_prefetch=1,
            grid=(2,),
            in_specs=[
                pl.BlockSpec((4, 2 * ROWS, TP_WIDTH), lambda i, o: (0, 0, 0)),
                pl.BlockSpec((32, 4, 48, UNIT_BLOCK), lambda i, o: (0, 0, 0, i)),
            ],
            out_specs=[pair] * 4,
            scratch_shapes=[pltpu.VMEM((4, 2 * ROWS, TP_WIDTH), F32)],
        ),
        compiler_params=pltpu.CompilerParams(vmem_limit_bytes=48 << 20),
        cost_estimate=pl.CostEstimate(
            flops=12 * ROWS * D * units, bytes_accessed=10 << 20, transcendentals=2 * ROWS * units
        ),
        name="feed_forward",
    )(place, x, weights)


def on_device(
    residual_in,
    query_rows,
    key_rows,
    value_rows,
    lengths,
    norm_gain,
    gate_weight,
    up_weight,
    down_weight,
):
    half = gate_weight.shape[1] // 2

    packed = jnp.concatenate([gate_weight, up_weight, down_weight.T], axis=0)
    halves = [packed[:, :half], packed[:, half:]]
    near = lax.all_to_all(jnp.stack(halves * 2), "yh", 0, 0)
    weights = lax.all_gather(near, ("x", "z"), axis=0)

    tail = jnp.broadcast_to(
        jnp.repeat(lengths.astype(BF16), 8)[:, None], (16, key_rows.shape[1])
    )
    k0 = jnp.concatenate([key_rows, tail], axis=0)
    k1, v1 = from_behind(k0, 1), from_behind(value_rows, 1)
    k2, v2 = from_behind(k1, 1), from_behind(v1, 1)

    attended, sent = attention(
        lengths, norm_gain[None, :], query_rows, k0, value_rows, k1, v1, k2, v2, residual_in
    )

    partner = swap(sent, "yh")
    parts = []
    for start in (sent, partner):
        chip = swap(start, "yl")
        parts += [start, swap(start, "c"), chip, swap(chip, "c")]
    own = 2 * lax.axis_index("yl") + lax.axis_index("c")
    place = jnp.stack([own, own ^ 1, own ^ 2, own ^ 3]).astype(jnp.int32)
    own_keep, own_send, partner_keep, partner_send = feed_forward(
        place, normalize(parts), weights
    )

    def add(left, right):
        return left.astype(F32) + right.astype(F32)

    partner_got = swap(partner_send, "c")
    own_got = swap(own_send, "c")
    partner_far = swap(add(partner_keep[0], partner_got[0]).astype(BF16), "yl")
    own_far = swap(add(own_keep[0], own_got[0]).astype(BF16), "yl")
    back = swap((add(partner_keep[1], partner_got[1]) + partner_far.astype(F32)).astype(BF16), "yh")
    summed = add(own_keep[1], own_got[1]) + own_far.astype(F32) + back.astype(F32)
    mixed = residual_in + attended.astype(F32) + summed
    return attended, mixed


def solution(mesh):
    fine = Mesh(mesh.devices.reshape(4, 8, 4, 2, 2), SEQ + TP)
    placed = (
        P(SEQ, TP),
        P(SEQ, TP),
        P(SEQ, TP),
        P(SEQ, TP),
        P(SEQ),
        P(TP),
        P(SEQ, TP),
        P(SEQ, TP),
        P(TP, SEQ),
    )
    return jax.shard_map(
        on_device,
        mesh=fine,
        in_specs=placed,
        out_specs=(P(SEQ, TP), P(SEQ, TP)),
        check_vma=False,
    )
```

```python
import math

import jax
import jax.numpy as jnp
from jax import lax
from jax.experimental import pallas as pl
from jax.experimental.pallas import tpu as pltpu
from jax.sharding import Mesh
from jax.sharding import PartitionSpec as P

D = 2048
HEAD_DIM = 128
SEG = 128
ROWS = 256
TP_WIDTH = 512
UNIT_BLOCK = 256
EXTRA = 16
epsilon = 1e-06

SEQ = ("x", "z", "yh")
TP = ("yl", "c")
F32 = jnp.float32
BF16 = jnp.bfloat16


def from_behind(value, by):
    size = lax.axis_size(SEQ)
    return lax.ppermute(value, SEQ, [(i, i + by) for i in range(size - by)])


def swap(value, axis):
    size = lax.axis_size(axis)
    return lax.ppermute(value, axis, [(i, i ^ 1) for i in range(size)])


def attention_kernel(
    lengths_ref, gain_ref, *refs
):
    outside, (att_ref, send_ref), inside, sems = refs[:8], refs[8:10], refs[10:18], refs[18]
    copies = [
        pltpu.make_async_copy(src, dst, sems.at[i])
        for i, (src, dst) in enumerate(zip(outside, inside))
    ]
    for copy in copies:
        copy.start()
    q_ref, k0_ref, v0_ref, k1_ref, v1_ref, k2_ref, v2_ref, res_ref = inside
    gain = gain_ref[...]
    high = gain.astype(BF16).astype(F32)
    middle = (gain - high).astype(BF16).astype(F32)
    low = gain - high - middle
    extra = lax.broadcasted_iota(jnp.int32, (EXTRA, TP_WIDTH), 0)
    extra = jnp.where(extra == 0, high, jnp.where(extra == 1, middle, jnp.where(extra == 2, low, 0.0)))
    send_ref[pl.ds(ROWS, EXTRA), :] = extra.astype(BF16)
    for copy in copies:
        copy.wait()
    rows = lax.broadcasted_iota(jnp.int32, (ROWS, ROWS), 0)
    cols = lax.broadcasted_iota(jnp.int32, (ROWS, ROWS), 1)
    col = lax.broadcasted_iota(jnp.int32, (1, ROWS), 1)

    def valid(key_ref):
        first = key_ref[pl.ds(ROWS, 8), pl.ds(0, ROWS)].astype(F32)[0:1, :].astype(jnp.int32)
        second = key_ref[pl.ds(ROWS + 8, 8), pl.ds(0, ROWS)].astype(F32)[0:1, :].astype(jnp.int32)
        return (col < jnp.where(col < SEG, first, second + SEG)).astype(jnp.int32)

    allowed = (
        (valid(k0_ref) > 0) & (cols <= rows),
        (valid(k1_ref) + jnp.zeros_like(cols)) > 0,
        (valid(k2_ref) > 0) & (cols > rows),
    )
    row = lax.broadcasted_iota(jnp.int32, (ROWS, 1), 0)
    keep = row < jnp.where(row < SEG, lengths_ref[0], lengths_ref[1] + SEG)
    scale = 1.0 / math.sqrt(HEAD_DIM)
    keys = (k0_ref, k1_ref, k2_ref)
    values = (v0_ref, v1_ref, v2_ref)
    for head in range(TP_WIDTH // HEAD_DIM):
        at = pl.ds(head * HEAD_DIM, HEAD_DIM)
        query = q_ref[:, at]
        masked = []
        for key_ref, allow in zip(keys, allowed):
            scores = lax.dot_general(
                query,
                key_ref[pl.ds(0, ROWS), at],
                (((1,), (1,)), ((), ())),
                preferred_element_type=F32,
            )
            masked.append(jnp.where(allow, scores * scale, -1e30))
        top = jnp.max(jnp.maximum(jnp.maximum(masked[0], masked[1]), masked[2]), axis=1, keepdims=True)
        weights = [jnp.where(a, jnp.exp(m - top), 0.0) for a, m in zip(allowed, masked)]
        denominator = jnp.sum(weights[0] + weights[1] + weights[2], axis=1, keepdims=True)
        numerator = jnp.zeros((ROWS, HEAD_DIM), F32)
        for weight, value_ref in zip(weights, values):
            numerator += jnp.dot(weight.astype(BF16), value_ref[:, at], preferred_element_type=F32)
        out = jnp.where(keep, numerator / jnp.where(keep, denominator, 1.0), 0.0).astype(BF16)
        att_ref[:, at] = out
        send_ref[pl.ds(0, ROWS), at] = (res_ref[:, at] + out.astype(F32)).astype(BF16)


HBM = pl.BlockSpec(memory_space=pltpu.HBM)
SMEM = pl.BlockSpec(memory_space=pltpu.SMEM)


def attention(lengths, gain, q, k0, v0, k1, v1, k2, v2, residual_in):
    return pl.pallas_call(
        attention_kernel,
        out_shape=(
            jax.ShapeDtypeStruct((ROWS, TP_WIDTH), BF16),
            jax.ShapeDtypeStruct((ROWS + EXTRA, TP_WIDTH), BF16),
        ),
        in_specs=[SMEM, pl.BlockSpec()] + [HBM] * 8,
        out_specs=(pl.BlockSpec(), pl.BlockSpec()),
        scratch_shapes=[
            pltpu.VMEM(a.shape, a.dtype) for a in (q, k0, v0, k1, v1, k2, v2, residual_in)
        ]
        + [pltpu.SemaphoreType.DMA((8,))],
        compiler_params=pltpu.CompilerParams(vmem_limit_bytes=60 << 20),
        cost_estimate=pl.CostEstimate(
            flops=4 * ROWS * 3 * ROWS * TP_WIDTH, bytes_accessed=3 << 20, transcendentals=3 << 18
        ),
        name="attention",
    )(lengths, gain, q, k0, v0, k1, v1, k2, v2, residual_in)


def normalize_kernel(*refs):
    parts, out = refs[:8], refs[8]
    for g in range(2):
        square = jnp.zeros((ROWS, 1), F32)
        for p in range(4):
            value = parts[4 * g + p][pl.ds(0, ROWS), :].astype(F32)
            square += jnp.sum(value * value, axis=1, keepdims=True)
        inverse = lax.rsqrt(square / D + epsilon)
        for p in range(4):
            extra = parts[4 * g + p][pl.ds(ROWS, EXTRA), :].astype(F32)
            gain = extra[0:1] + extra[1:2] + extra[2:3]
            value = parts[4 * g + p][pl.ds(0, ROWS), :].astype(F32)
            out[p, pl.ds(g * ROWS, ROWS), :] = (value * inverse * gain).astype(BF16)


def normalize(parts):
    return pl.pallas_call(
        normalize_kernel,
        out_shape=jax.ShapeDtypeStruct((4, 2 * ROWS, TP_WIDTH), BF16),
        compiler_params=pltpu.CompilerParams(vmem_limit_bytes=32 << 20),
        cost_estimate=pl.CostEstimate(flops=8 * ROWS * D, bytes_accessed=4 << 20, transcendentals=0),
        name="normalize",
    )(*parts)


def feed_forward_kernel(place_ref, x_ref, w_ref, *refs):
    outs, acc_ref = refs[:4], refs[4]
    step = pl.program_id(0)

    def block(p, kind):
        pieces = [
            w_ref[
                pl.ds(place_ref[p] * 8, 8),
                pl.ds(y, 1),
                pl.ds(kind * 16, 16),
                :,
            ]
            for y in range(4)
        ]
        return jnp.concatenate(pieces, axis=1).reshape(TP_WIDTH, UNIT_BLOCK)

    gate = jnp.zeros((2 * ROWS, UNIT_BLOCK), F32)
    up = jnp.zeros((2 * ROWS, UNIT_BLOCK), F32)
    for p in range(4):
        gate += jnp.dot(x_ref[p], block(p, 0), preferred_element_type=F32)
        up += jnp.dot(x_ref[p], block(p, 1), preferred_element_type=F32)
    hidden = (gate / (1.0 + jnp.exp(-gate)) * up).astype(BF16)

    def down(p):
        return lax.dot_general(
            hidden, block(p, 2), (((1,), (1,)), ((), ())), preferred_element_type=F32
        )

    @pl.when(step == 0)
    def _():
        for p in range(4):
            acc_ref[p] = down(p)

    @pl.when(step == 1)
    def _():
        for i, p in enumerate((2, 0)):
            for away in range(2):
                total = (acc_ref[p + away] + down(p + away)).astype(BF16)
                for g in range(2):
                    outs[2 * g + away][i] = total[g * ROWS : (g + 1) * ROWS]


def feed_forward(place, x, weights):
    pair = pl.BlockSpec((2, ROWS, TP_WIDTH), lambda i, o: (0, 0, 0))
    units = weights.shape[3]
    assert units == 2 * UNIT_BLOCK
    return pl.pallas_call(
        feed_forward_kernel,
        out_shape=[jax.ShapeDtypeStruct((2, ROWS, TP_WIDTH), BF16)] * 4,
        grid_spec=pltpu.PrefetchScalarGridSpec(
            num_scalar_prefetch=1,
            grid=(2,),
            in_specs=[
                pl.BlockSpec((4, 2 * ROWS, TP_WIDTH), lambda i, o: (0, 0, 0)),
                pl.BlockSpec((32, 4, 48, UNIT_BLOCK), lambda i, o: (0, 0, 0, i)),
            ],
            out_specs=[pair] * 4,
            scratch_shapes=[pltpu.VMEM((4, 2 * ROWS, TP_WIDTH), F32)],
        ),
        compiler_params=pltpu.CompilerParams(vmem_limit_bytes=48 << 20),
        cost_estimate=pl.CostEstimate(
            flops=12 * ROWS * D * units, bytes_accessed=10 << 20, transcendentals=2 * ROWS * units
        ),
        name="feed_forward",
    )(place, x, weights)


def on_device(
    residual_in,
    query_rows,
    key_rows,
    value_rows,
    lengths,
    norm_gain,
    gate_weight,
    up_weight,
    down_weight,
):
    half = gate_weight.shape[1] // 2

    packed = jnp.concatenate([gate_weight, up_weight, down_weight.T], axis=0)
    halves = [packed[:, :half], packed[:, half:]]
    near = lax.all_to_all(jnp.stack(halves * 2), "yh", 0, 0)
    weights = lax.all_gather(near, ("x", "z"), axis=0)

    tail = jnp.broadcast_to(
        jnp.repeat(lengths.astype(BF16), 8)[:, None], (16, key_rows.shape[1])
    )
    k0 = jnp.concatenate([key_rows, tail], axis=0)
    k1, v1 = from_behind(k0, 1), from_behind(value_rows, 1)
    k2, v2 = from_behind(k1, 1), from_behind(v1, 1)

    attended, sent = attention(
        lengths, norm_gain[None, :], query_rows, k0, value_rows, k1, v1, k2, v2, residual_in
    )

    partner = swap(sent, "yh")
    parts = []
    for start in (sent, partner):
        chip = swap(start, "yl")
        parts += [start, swap(start, "c"), chip, swap(chip, "c")]
    own = 2 * lax.axis_index("yl") + lax.axis_index("c")
    place = jnp.stack([own, own ^ 1, own ^ 2, own ^ 3]).astype(jnp.int32)
    own_keep, own_send, partner_keep, partner_send = feed_forward(
        place, normalize(parts), weights
    )

    def add(left, right):
        return left.astype(F32) + right.astype(F32)

    partner_got = swap(partner_send, "c")
    own_got = swap(own_send, "c")
    partner_far = swap(add(partner_keep[0], partner_got[0]).astype(BF16), "yl")
    back = (add(partner_keep[1], partner_got[1]) + partner_far.astype(F32)).astype(BF16)
    own_far = add(own_keep[0], own_got[0]).astype(BF16)
    back, own_far = lax.optimization_barrier((back, own_far))
    back = swap(back, "yh")
    own_far = swap(own_far, "yl")
    summed = add(own_keep[1], own_got[1]) + own_far.astype(F32) + back.astype(F32)
    mixed = residual_in + attended.astype(F32) + summed
    return attended, mixed


def solution(mesh):
    fine = Mesh(mesh.devices.reshape(4, 8, 4, 2, 2), SEQ + TP)
    placed = (
        P(SEQ, TP),
        P(SEQ, TP),
        P(SEQ, TP),
        P(SEQ, TP),
        P(SEQ),
        P(TP),
        P(SEQ, TP),
        P(SEQ, TP),
        P(TP, SEQ),
    )
    return jax.shard_map(
        on_device,
        mesh=fine,
        in_specs=placed,
        out_specs=(P(SEQ, TP), P(SEQ, TP)),
        check_vma=False,
    )
```
